128 devices in a mesh: row: 16 (over x, y), col: 8 (over z, core).
Axes of the slice: x: 4, y: 4, z: 4, core: 2. Of those that a mesh axis runs over, the one named last changes fastest.
Arguments:
- child_tiles: float32 [14336, 256, 128], P(('row', 'col')), may hold values from -2.5 to 2.5
- tile_dest: int32 [14336], P(('row', 'col')), may hold values from 0 to 6143, as said below
- tile_mask: int32 [14336, 256], P(('row', 'col')), may hold values 0 or 1
- tile_count: int32 [128], P(('row', 'col')), may hold values from 84 to 112, as said below
- front_diagonal: float32 [2, 2048], P(None, 'col'), may hold values from 200 to 400
Outputs:
- front_out: float32 [49152, 2, 2048], P('row', None, 'col')
The draws below stay inside these ranges and needn't reach their ends.
Inputs may be any that keep to these rules, and one draw needn't show every extreme that they name: tile_dest[i] = r * 32 + t names front rows r * 256 onward and slab columns t * 128 onward; of the 112 tiles of one device at most 2 name tiles that lie on any one device of front_out's placement, and that most is reached. Tile i * 112 + m is live when m < tile_count[i].
All inputs are finite; a program needn't handle non-finite values. No bound on the sum of `tile_mask` on one device may be relied on, other than what follows from the above.
Results may differ from the reference program's by a relative error of at most 0.0001.
Values sent between devices are 32-bit elements; how exact they have to be, the bound alone decides.
No kernel may reach another device: no remote copies, remote signals or barrier semaphores. Data moves between devices by JAX's collectives and lax.ppermute only.
A program may use at most 192 MiB of HBM per device.

```python
import jax
import jax.numpy as jnp
from jax import lax

NF = 49152
PB = 256
TR = 256
CAP = 2
CB = 2
TC = 128
NCT = 32
KT = 112
N_ROW = 16
N_COL = 8
DEVICES = 128


def draw_tile_dest(key, part):
    base_key = jax.random.fold_in(key, 11)
    k_hot, k_pick, k_row, k_blk, k_half = jax.random.split(base_key, 5)
    slot_count = DEVICES * CAP
    heavy_set = jax.random.permutation(k_hot, DEVICES)[:DEVICES // 8]
    heavy_flag = jnp.zeros((DEVICES,), jnp.int32).at[heavy_set].set(1)
    slot_owner = jnp.arange(slot_count, dtype=jnp.int32) // CAP
    scores = jax.random.randint(k_pick, (DEVICES, slot_count), 0, 4096) + heavy_flag[slot_owner][None, :] * 4096
    scores = scores * slot_count + jnp.arange(slot_count, dtype=jnp.int32)[None, :]
    chosen = lax.top_k(scores, KT)[1]
    owner_dev = chosen // CAP
    owner_row = owner_dev // N_COL
    owner_col = owner_dev % N_COL
    row_tiles = NF // (N_ROW * TR)
    row_tile = owner_row * row_tiles + jax.random.randint(k_row, (DEVICES, KT), 0, row_tiles)
    col_block = owner_col + N_COL * jax.random.randint(k_blk, (DEVICES, KT), 0, CB)
    col_half = jax.random.randint(k_half, (DEVICES, KT), 0, PB // TC)
    result = row_tile * NCT + col_block * (PB // TC) + col_half
    return result.reshape(DEVICES * KT).astype(jnp.int32)


def draw_tile_count(key, part):
    base_key = jax.random.fold_in(key, 23)
    k_count, k_full = jax.random.split(base_key, 2)
    counts = jax.random.randint(k_count, (DEVICES,), 3 * KT // 4, KT + 1)
    full_at = jax.random.randint(k_full, (), 0, DEVICES)
    return counts.at[full_at].set(KT).astype(jnp.int32)


def touch_ends(entries, rng, smallest, high):
    longest = entries.shape.index(max(entries.shape))
    spots = []
    for shift in (0, 1):
        where = [jax.random.randint(jax.random.fold_in(rng, axis), (), 0, length) for axis, length in enumerate(entries.shape)]
        where[longest] = (where[longest] + shift) % entries.shape[longest]
        spots.append(tuple(where))
    return entries.at[spots[0]].set(smallest).at[spots[1]].set(high)


def level_of(own_key, dims, pieces, low, largest):
    def one(dim, parts):
        heights = jax.random.uniform(jax.random.fold_in(jax.random.fold_in(own_key, 6), dim), (parts,), jnp.float32, low / len(pieces), largest / len(pieces))
        return jnp.repeat(jnp.exp(heights), dims[dim] // parts).reshape((-1,) + (1,) * (len(dims) - dim - 1))

    factor_of = one(*pieces[0])
    for cut in pieces[1:]:
        factor_of = factor_of * one(*cut)
    return factor_of


def gaussian(own_key, extent, deviation, most, pieces=(), kind=jnp.bfloat16):
    values = deviation * jax.random.normal(own_key, extent, jnp.float32)
    if pieces:
        values = values * level_of(own_key, extent, pieces, -0.22, 0.18)
    return jnp.clip(values, -most, most).astype(kind)


def setup_inputs(seed: int = 0) -> dict:
    keys = jax.random.split(jax.random.key(seed), 6)
    child_tiles = gaussian(keys[0], (DEVICES * KT, TR, TC), 1.0, 2.5, ((0, 128),), jnp.float32)
    tile_dest = draw_tile_dest(jax.random.fold_in(keys[5], 71), 0)
    tile_mask = touch_ends((jax.random.randint(keys[2], (DEVICES * KT, TR), 0, 4) < 3).astype(jnp.int32), jax.random.fold_in(keys[2], 1), 0, 1)
    tile_count = draw_tile_count(jax.random.fold_in(keys[5], 71), 0)
    front_diagonal = jnp.clip(200.0 + 200.0 * jax.random.uniform(keys[4], (CB, N_COL * PB), jnp.float32) ** level_of(keys[4], (CB, N_COL * PB), ((1, 8),), -0.2, 0.2), 200.0, 400.0)
    return dict(child_tiles=child_tiles, tile_dest=tile_dest, tile_mask=tile_mask, tile_count=tile_count, front_diagonal=front_diagonal)


def reference(child_tiles, tile_dest, tile_mask, tile_count, front_diagonal):
    col_tiles = CB * N_COL * PB // TC
    tile_total = NF // TR * col_tiles
    width = col_tiles * TC
    positions = jnp.arange(DEVICES * KT, dtype=jnp.int32)
    is_live = positions % KT < tile_count[positions // KT]
    targets = jnp.where(is_live, tile_dest, tile_total).astype(jnp.int32)
    masked = child_tiles * tile_mask.astype(jnp.float32)[:, :, None]
    summed = jax.ops.segment_sum(masked, targets, num_segments=tile_total + 1)[:tile_total]
    assembled = summed.reshape(NF // TR, col_tiles, TR, TC).transpose(0, 2, 1, 3).reshape(NF, width)
    diag_flat = front_diagonal.reshape(width)
    columns = jnp.arange(width, dtype=jnp.int32)
    assembled = assembled.at[columns, columns].add(diag_flat)
    row_ids = jnp.arange(NF, dtype=jnp.int32)[:, None]
    for section in range(2):
        lower_edge = section * PB
        upper_edge = lower_edge + PB
        pivot = assembled[lower_edge:upper_edge, lower_edge:upper_edge]
        factor = jnp.linalg.cholesky(0.5 * (pivot + pivot.T))
        panel_raw = assembled[:, lower_edge:upper_edge]
        solved = jax.scipy.linalg.solve_triangular(factor, panel_raw.T, lower=True).T
        lower_panel = jnp.where(row_ids < lower_edge, jnp.zeros_like(solved), solved)
        lower_panel = lower_panel.at[lower_edge:upper_edge].set(factor)
        update_term = jnp.dot(lower_panel, lower_panel[upper_edge:width].T, precision=lax.Precision.HIGHEST)
        assembled = assembled.at[:, upper_edge:].add(-update_term)
        assembled = assembled.at[:, lower_edge:upper_edge].set(lower_panel)
    return assembled.reshape(NF, CB, N_COL * PB)
```

```python
import jax
import jax.numpy as jnp
from jax import lax
from jax.experimental import pallas as pl
from jax.experimental.pallas import tpu as pltpu
from jax.sharding import PartitionSpec as P

NF = 49152
EARLY = 8
GROUP = 8
CHUNKS = (56, 48)
BULK = 2**31
HIGHEST = lax.Precision.HIGHEST
VMEM_BYTES = 56 * 1024 * 1024


def pack_tiles(order, child_tiles, mask_columns, first, count, meta=None):
    tile_rows, tile_cols = child_tiles.shape[1:]
    stripes = tile_rows // 2
    base = first // GROUP
    extra = 0 if meta is None else meta.shape[0]
    width = 2 * GROUP + extra

    def body(order_ref, *refs):
        tiles, mask_ref = refs[:GROUP], refs[GROUP]
        out_ref, rows_ref = refs[-2], refs[-1]
        for i in range(GROUP):
            for s in range(2):
                rows = tiles[i][0, s * stripes : (s + 1) * stripes, :]
                column = mask_ref[0, s * stripes : (s + 1) * stripes, i : i + 1]
                rows_ref[pl.ds(2 * i + s, stripes, stride=2 * GROUP), :] = rows * column
        out_ref[:, : 2 * GROUP, :] = rows_ref[...].reshape(stripes, 2 * GROUP, tile_cols)
        if extra:
            meta_ref = refs[GROUP + 1]
            out_ref[:, 2 * GROUP :, :] = jnp.broadcast_to(
                meta_ref[...][None], (stripes, extra, tile_cols)
            )

    def tile_spec(i):
        return pl.BlockSpec(
            (1, tile_rows, tile_cols), lambda g, order_ref: (order_ref[first + g * GROUP + i], 0, 0)
        )

    in_specs = [tile_spec(i) for i in range(GROUP)]
    in_specs.append(pl.BlockSpec((1, tile_rows, GROUP), lambda g, order_ref: (base + g, 0, 0)))
    operands = [child_tiles] * GROUP + [mask_columns]
    if extra:
        in_specs.append(pl.BlockSpec((extra, tile_cols), lambda g, order_ref: (0, 0)))
        operands.append(meta)
    steps = count // GROUP
    return pl.pallas_call(
        body,
        grid_spec=pltpu.PrefetchScalarGridSpec(
            num_scalar_prefetch=1,
            grid=(steps,),
            in_specs=in_specs,
            out_specs=pl.BlockSpec((stripes, width, tile_cols), lambda g, order_ref: (0, g, 0)),
            scratch_shapes=[pltpu.VMEM((stripes * 2 * GROUP, tile_cols), jnp.float32)],
        ),
        out_shape=jax.ShapeDtypeStruct((stripes, steps * width, tile_cols), jnp.float32),
        compiler_params=pltpu.CompilerParams(vmem_limit_bytes=VMEM_BYTES),
        name="pack_tiles",
    )(order, *operands)


def add_pieces(targets, pieces, early, sums, first, weight):
    sources, count, two, lanes = pieces.shape
    n_sums = 6144
    per_step = 8
    fresh = sums is None

    def body(target_ref, pieces_ref, *refs):
        sums_ref = refs[-1]
        step = pl.program_id(0)

        @pl.when(step == 0)
        def _():
            sums_ref[...] = jnp.zeros_like(sums_ref) if fresh else refs[0][...]

        for n in range(per_step):
            source = step * per_step + n
            if fresh:
                for i in range(EARLY):
                    d = target_ref[source, i]
                    sums_ref[d] = sums_ref[d] + refs[0][n, i]
            for at in range(0, count, GROUP):
                ds = [target_ref[source, first + at + i] for i in range(GROUP)]
                news = [sums_ref[ds[i]] + pieces_ref[n, at + i] for i in range(GROUP)]
                for i in range(GROUP):
                    sums_ref[ds[i]] = news[i]

    def streamed(x):
        return pl.BlockSpec((per_step,) + x.shape[1:], lambda g, target_ref: (g, 0, 0, 0))

    whole = pl.BlockSpec(
        (n_sums, two, lanes), lambda g, target_ref: (0, 0, 0), pipeline_mode=pl.Buffered(1)
    )
    return pl.pallas_call(
        body,
        grid_spec=pltpu.PrefetchScalarGridSpec(
            num_scalar_prefetch=1,
            grid=(sources // per_step,),
            in_specs=[streamed(pieces), streamed(early) if fresh else whole],
            out_specs=whole,
        ),
        out_shape=jax.ShapeDtypeStruct((n_sums, two, lanes), jnp.float32),
        compiler_params=pltpu.CompilerParams(vmem_limit_bytes=VMEM_BYTES),
        cost_estimate=pl.CostEstimate(flops=weight, transcendentals=0, bytes_accessed=weight),
        name="add_pieces",
    )(targets, pieces, early if fresh else sums)


def add_top(spots, pieces, n_sums):
    sources, pitch, two, lanes = pieces.shape
    slots = spots.shape[1]

    def body(spot_ref, pieces_ref, out_ref, *parts):
        for part in parts:
            part[...] = jnp.zeros_like(part)

        def one(source, _):
            for i in range(slots):
                d = spot_ref[source, i]
                parts[i][d] = parts[i][d] + pieces_ref[source, i]
            return 0

        lax.fori_loop(0, sources, one, 0, unroll=4)
        total = parts[0][:n_sums]
        for part in parts[1:]:
            total = total + part[:n_sums]
        out_ref[...] = total

    return pl.pallas_call(
        body,
        grid_spec=pltpu.PrefetchScalarGridSpec(
            num_scalar_prefetch=1,
            grid=(1,),
            in_specs=[pl.BlockSpec(pieces.shape, lambda g, spot_ref: (0, 0, 0, 0))],
            out_specs=pl.BlockSpec((n_sums, two, lanes), lambda g, spot_ref: (0, 0, 0)),
            scratch_shapes=[pltpu.VMEM((n_sums + 8, two, lanes), jnp.float32)] * slots,
        ),
        out_shape=jax.ShapeDtypeStruct((n_sums, two, lanes), jnp.float32),
        compiler_params=pltpu.CompilerParams(vmem_limit_bytes=VMEM_BYTES),
        name="add_top",
    )(spots, pieces)


def factor_corner(corner, diagonal):
    size = corner.shape[2]
    n = 4

    def dot(a, b, transposed):
        dims = (((1,), (1 if transposed else 0,)), ((), ()))
        return lax.dot_general(a, b, dims, precision=HIGHEST, preferred_element_type=jnp.float32)

    def eliminate(block):
        groups = [block[8 * g : 8 * g + 8, :] for g in range(size // 8)]
        lane = lax.broadcasted_iota(jnp.int32, (8, size), 1)
        sub = lax.broadcasted_iota(jnp.int32, (8, size), 0)
        for p in range(size // 8):
            j0 = 8 * p
            rows = [jnp.broadcast_to(groups[p][r : r + 1, :], (8, size)) for r in range(8)]
            entry = [
                [
                    jnp.broadcast_to(rows[r][:, j0 + c : j0 + c + 1], (8, size)) if c >= r else None
                    for c in range(8)
                ]
                for r in range(8)
            ]
            ratio = [[None] * 8 for _ in range(8)]
            scaled = []
            done = groups[p]
            for r in range(8):
                row = jnp.where(jnp.logical_and(lane >= j0, lane < j0 + r), 0.0, rows[r])
                for q in range(r):
                    settled = jnp.logical_and(lane > j0 + q, lane < j0 + r)
                    row = row - ratio[r][q] * jnp.where(settled, 0.0, rows[q])
                done = jnp.where(sub == r, row, done)
                rows[r] = jnp.where(lane == j0 + r, 1.0, row)
                inverse = 1.0 / entry[r][r]
                settled = jnp.logical_and(lane > j0 + r, lane < j0 + 8)
                scaled.append(jnp.where(settled, 0.0, rows[r]) * inverse)
                for c in range(r + 1, 8):
                    ratio[c][r] = entry[r][c] * inverse
                for c in range(r + 1, 8):
                    for d in range(c, 8):
                        entry[c][d] = entry[c][d] - ratio[c][r] * entry[r][d]
            groups[p] = done
            inside = jnp.logical_and(lane >= j0, lane < j0 + 8)
            for g in range(p + 1, size // 8):
                columns = []
                result = jnp.where(inside, 0.0, groups[g])
                for c in range(8):
                    column = jnp.broadcast_to(groups[g][:, j0 + c : j0 + c + 1], (8, size))
                    for q in range(c):
                        column = column - ratio[c][q] * columns[q]
                    columns.append(column)
                    result = result - column * scaled[c]
                groups[g] = result
        return jnp.concatenate(groups, axis=0)

    def body(corner_ref, diag_ref, lower_ref, inverse_ref, flat_ref, a_ref, l_ref, i_ref):
        row = lax.broadcasted_iota(jnp.int32, (size, size), 0)
        col = lax.broadcasted_iota(jnp.int32, (size, size), 1)
        flat_ref[...] = corner_ref[...].reshape(size * 16, size)

        def raw(q, t):
            block = flat_ref[pl.ds(t * 4 + q, size, stride=16), :]
            if q == t:
                block = block + jnp.where(row == col, diag_ref[t : t + 1, :], 0.0)
            return block

        for q in range(n):
            for t in range(q + 1):
                block = raw(q, t)
                if q // 2 == t // 2:
                    block = 0.5 * (block + raw(t, q).T)
                a_ref[q * n + t] = block

        def step(k, _):
            done = eliminate(a_ref[k * n + k])
            pivots = jnp.sum(jnp.where(row == col, done, 0.0), axis=1, keepdims=True)
            root = jnp.sqrt(pivots)
            upper = jnp.where(col >= row, done, 0.0) / root
            inv = jnp.where(col < row, done, jnp.where(col == row, 1.0, 0.0)) / root
            l_ref[k * n + k] = upper.T
            i_ref[k * n + k] = inv
            for i in range(1, n):

                @pl.when(i > k)
                def _():
                    l_ref[i * n + k] = dot(a_ref[i * n + k], inv, True)

            for i in range(1, n):
                for j in range(1, i + 1):

                    @pl.when(j > k)
                    def _():
                        a_ref[i * n + j] = a_ref[i * n + j] - dot(
                            l_ref[i * n + k], l_ref[j * n + k], True
                        )

            return 0

        lax.fori_loop(0, n, step, 0)
        for i in range(n):
            for j in range(i):
                total = dot(l_ref[i * n + j], i_ref[j * n + j], False)
                for k in range(j + 1, i):
                    total = total + dot(l_ref[i * n + k], i_ref[k * n + j], False)
                i_ref[i * n + j] = -dot(i_ref[i * n + i], total, False)
        zero = jnp.zeros((size, size), jnp.float32)
        for i in range(n):
            for j in range(n):
                rows, cols = slice(i * size, (i + 1) * size), slice(j * size, (j + 1) * size)
                lower_ref[rows, cols] = l_ref[i * n + j] if j <= i else zero
                inverse_ref[rows, cols] = i_ref[i * n + j] if j <= i else zero

    shape = jax.ShapeDtypeStruct((n * size, n * size), jnp.float32)
    blocks = pltpu.VMEM((n * n, size, size), jnp.float32)
    return pl.pallas_call(
        body,
        out_shape=(shape, shape),
        scratch_shapes=[pltpu.VMEM((size * 16, size), jnp.float32), blocks, blocks, blocks],
        compiler_params=pltpu.CompilerParams(vmem_limit_bytes=VMEM_BYTES),
        name="factor_corner",
    )(corner, diagonal)


def update_rows(sums, top, inverse, own_rows, diagonal):
    blocks, n_col, halves, n_rows, lanes = sums.shape
    stripes, top_cols, _, _ = top.shape
    near = top_cols * lanes
    n_row = stripes // n_col
    share = n_rows // 2 // n_row
    pair = 8 // (blocks * halves)

    def dot(a, b, transposed):
        dims = (((1,), (1 if transposed else 0,)), ((), ()))
        return lax.dot_general(a, b, dims, precision=HIGHEST, preferred_element_type=jnp.float32)

    def body(
        sums_ref,
        panel_in_ref,
        top_ref,
        inverse_ref,
        own_ref,
        diag_ref,
        out_ref,
        panel_ref,
        factor_ref,
        flat_ref,
        result_ref,
        mixed_ref,
    ):
        g = pl.program_id(0)
        n_diag = diag_ref.shape[0]
        row = lax.broadcasted_iota(jnp.int32, (n_diag, lanes), 0)

        def with_diagonal(x, t):
            head = x[:n_diag] + jnp.where(row == t, diag_ref[...], 0.0)
            return jnp.concatenate([head, x[n_diag:]], axis=0)

        @pl.when(g == 0)
        def _():
            x = jnp.concatenate(
                [with_diagonal(panel_in_ref[0, t // 2, t % 2], t) for t in range(top_cols)], axis=1
            )
            panel = dot(x, inverse_ref[...], True)
            at = lax.broadcasted_iota(jnp.int32, (8, near), 0)
            head = jnp.where(at < 4, own_ref[...], panel[:8])
            panel = jnp.concatenate([head, panel[8:]], axis=0)
            panel_ref[...] = panel
            factor_ref[...] = dot(panel, inverse_ref[...], False)

        flat_ref[...] = top_ref[...].reshape(stripes * top_cols * 8, lanes)
        for i in range(pair):
            c = g * pair + i
            for cb in range(blocks):
                weights = jnp.concatenate(
                    [
                        jnp.concatenate(
                            [
                                flat_ref[
                                    pl.ds(
                                        k * 8 + (i * blocks + cb) * halves + h,
                                        stripes,
                                        stride=top_cols * 8,
                                    ),
                                    :,
                                ]
                                for k in range(top_cols)
                            ],
                            axis=1,
                        )
                        for h in range(halves)
                    ],
                    axis=0,
                )
                product = dot(factor_ref[...], weights, True)
                for h in range(halves):
                    t = (cb * n_col + c) * halves + h
                    result = with_diagonal(sums_ref[cb, i, h], t)
                    result = result - product[:, h * lanes : (h + 1) * lanes]
                    if cb == 0:
                        at = (i * halves + h) * lanes
                        result = jnp.where(g == 0, panel_ref[:, at : at + lanes], result)
                    result_ref[...] = result
                    for s in range(2):
                        mixed_ref[pl.ds(s * 4 + h * 2 + cb, n_rows // 2, stride=8), :] = result_ref[
                            pl.ds(s, n_rows // 2, stride=2), :
                        ]
            out_ref[:, i] = mixed_ref[...].reshape(n_row, share * 8, lanes)

    def fixed(*shape):
        return pl.BlockSpec(shape, lambda g: (0,) * len(shape))

    return pl.pallas_call(
        body,
        grid=(n_col // pair,),
        in_specs=[
            pl.BlockSpec((blocks, pair, halves, n_rows, lanes), lambda g: (0, g, 0, 0, 0)),
            pl.BlockSpec((1, 2, halves, n_rows, lanes), lambda g: (0, 0, 0, 0, 0)),
            pl.BlockSpec((stripes, top_cols, 8, lanes), lambda g: (0, 0, g, 0)),
            fixed(near, near),
            fixed(8, near),
            fixed(*diagonal.shape),
        ],
        out_specs=pl.BlockSpec((n_row, pair, share * 8, lanes), lambda g: (0, g, 0, 0)),
        out_shape=jax.ShapeDtypeStruct((n_row, n_col, share * 8, lanes), jnp.float32),
        scratch_shapes=[
            pltpu.VMEM((n_rows, near), jnp.float32),
            pltpu.VMEM((n_rows, near), jnp.float32),
            pltpu.VMEM((stripes * top_cols * 8, lanes), jnp.float32),
            pltpu.VMEM((n_rows, lanes), jnp.float32),
            pltpu.VMEM((n_rows * 4, lanes), jnp.float32),
        ],
        compiler_params=pltpu.CompilerParams(vmem_limit_bytes=VMEM_BYTES),
        name="update_rows",
    )(sums, sums, top, inverse, own_rows, diagonal)


def place_rows(received):
    stripes, width, lanes = received.shape
    row_tiles = width // 8

    def body(in_ref, out_ref, flat_ref):
        flat_ref[...] = in_ref[...].reshape(stripes * 8, lanes)
        for s in range(2):
            for k in range(4):
                out_ref[pl.ds(s * stripes * 4 + k, stripes, stride=4), :] = flat_ref[
                    pl.ds(s * 4 + k, stripes, stride=8), :
                ]

    return pl.pallas_call(
        body,
        grid=(row_tiles,),
        in_specs=[pl.BlockSpec((stripes, 8, lanes), lambda g: (0, g, 0))],
        out_specs=pl.BlockSpec((stripes * 8, lanes), lambda g: (g, 0)),
        out_shape=jax.ShapeDtypeStruct((row_tiles * stripes * 8, lanes), jnp.float32),
        scratch_shapes=[pltpu.VMEM((stripes * 8, lanes), jnp.float32)],
        compiler_params=pltpu.CompilerParams(vmem_limit_bytes=VMEM_BYTES),
        name="place_rows",
    )(received)


def tile_order(tile_dest, col_tiles, top_rows, top_cols):
    total = tile_dest.shape[0]
    ids = jnp.arange(total, dtype=jnp.int32)
    same = tile_dest[:, None] == tile_dest[None, :]
    first_of = jnp.min(jnp.where(same, ids[None, :], total), axis=1)
    later = jnp.any(jnp.logical_and(same, ids[None, :] > ids[:, None]), axis=1)
    top = jnp.logical_and(tile_dest // col_tiles < top_rows, tile_dest % col_tiles < top_cols)
    rest = jnp.where(
        first_of < ids, 3 * total + first_of, jnp.where(later, total + ids, 2 * total + ids)
    )
    key = jnp.where(top, ids, rest)
    position = jnp.sum((key[None, :] < key[:, None]).astype(jnp.int32), axis=1)
    return (position[:, None] == ids[None, :]).astype(jnp.int32)


def on_device(child_tiles, tile_dest, tile_mask, tile_count, front_diagonal):
    axes = ("row", "col")
    n_row = lax.axis_size("row")
    n_col = lax.axis_size("col")
    devices = n_row * n_col
    me = lax.axis_index("row") * n_col + lax.axis_index("col")
    tile_total, tile_rows, lanes = child_tiles.shape
    col_blocks, panel = front_diagonal.shape
    halves = panel // lanes
    row_tiles = NF // tile_rows
    col_tiles = col_blocks * n_col * halves
    width = col_tiles * lanes
    top_rows = width // tile_rows
    top_cols = 2 * halves

    placed = tile_order(tile_dest, col_tiles, top_rows, top_cols)
    ids = jnp.arange(tile_total, dtype=jnp.int32)
    target = (tile_dest % col_tiles) * row_tiles + tile_dest // col_tiles
    order = jnp.sum(placed * ids[:, None], axis=0)
    target_sent = jnp.sum(placed * target[:, None], axis=0)
    live = (ids < tile_count[0]).astype(jnp.float32)
    mask_columns = lax.dot_general(
        tile_mask.astype(jnp.float32),
        placed.astype(jnp.float32) * live[:, None],
        (((0,), (0,)), ((), ())),
    )
    mask_columns = mask_columns.reshape(tile_rows, tile_total // GROUP, GROUP).transpose(1, 0, 2)
    meta = jnp.concatenate(
        [
            jnp.pad(target_sent.astype(jnp.float32), (0, lanes - tile_total))[None],
            front_diagonal.reshape(col_blocks * halves, lanes),
            jnp.zeros((8 - 1 - col_blocks * halves, lanes), jnp.float32),
        ],
        axis=0,
    )

    def exchange(x):
        return lax.all_to_all(x, axes, split_axis=0, concat_axis=0, tiled=True)

    early = exchange(pack_tiles(order, child_tiles, mask_columns, 0, EARLY, meta))
    at = EARLY
    first_pack = pack_tiles(order, child_tiles, mask_columns, at, CHUNKS[0])
    early, first_pack = lax.optimization_barrier((early, first_pack))
    received0 = exchange(first_pack)

    targets = early[:, 2 * EARLY, :].astype(jnp.int32)
    diagonal = early[:n_col, 2 * EARLY + 1 : 2 * EARLY + 1 + col_blocks * halves, :]
    diagonal = diagonal.reshape(n_col, col_blocks, panel).transpose(1, 0, 2)
    diagonal = diagonal.reshape(col_tiles, lanes)
    early = early.reshape(devices, EARLY + 4, 2, lanes)
    n_top = top_cols * top_rows
    tile, row = targets[:, :EARLY] // row_tiles, targets[:, :EARLY] % row_tiles
    spots = tile * top_rows + row % n_col * col_blocks + row // n_col
    spots = jnp.where(jnp.logical_and(tile < top_cols, row < top_rows), spots, n_top)
    view = add_top(spots, early, n_top)
    top = lax.all_gather(view.reshape(top_cols, 2 * top_rows, lanes), "col")
    top = lax.all_gather(top, "row").reshape(devices, top_cols, 2 * top_rows, lanes)

    second_pack = pack_tiles(order, child_tiles, mask_columns, at + CHUNKS[0], CHUNKS[1])
    received0, second_pack = lax.optimization_barrier((received0, second_pack))
    received1 = exchange(second_pack)
    pieces = received0.reshape(devices, CHUNKS[0], 2, lanes)
    sums = add_pieces(targets, pieces, early, None, at, BULK)
    top, sums = lax.optimization_barrier((top, sums))
    corner = top.reshape(devices, top_cols, n_col, col_blocks, 2, lanes)[:, :, :2, 0]
    lower, inverse = factor_corner(corner.reshape(devices, 4 * top_cols, lanes), diagonal[:8])
    own_rows = lax.dynamic_slice(
        lower.reshape(top_cols, devices, top_cols * lanes),
        (0, me, 0),
        (top_cols, 1, top_cols * lanes),
    )
    own_rows = jnp.pad(own_rows.reshape(top_cols, top_cols * lanes), ((0, 8 - top_cols), (0, 0)))
    received1, inverse, own_rows = lax.optimization_barrier((received1, inverse, own_rows))
    pieces = received1.reshape(devices, CHUNKS[1], 2, lanes)
    sums = add_pieces(targets, pieces, None, sums, at + CHUNKS[0], BULK)

    own = jnp.where(jnp.arange(lanes, dtype=jnp.int32)[None, :] == me, diagonal, 0.0)
    result = update_rows(
        sums.reshape(col_blocks, n_col, halves, 2 * row_tiles, lanes), top, inverse, own_rows, own
    )
    received = exchange(result.reshape(devices, -1, lanes))
    rows = place_rows(received)
    rows = rows.reshape(NF // n_row, halves, col_blocks, lanes).transpose(0, 2, 1, 3)
    return rows.reshape(NF // n_row, col_blocks, panel)


def solution(mesh):
    in_specs = (
        P(("row", "col"), None, None),
        P(("row", "col")),
        P(("row", "col"), None),
        P(("row", "col")),
        P(None, "col"),
    )
    out_specs = P("row", None, "col")
    return jax.shard_map(
        on_device, mesh=mesh, in_specs=in_specs, out_specs=out_specs, check_vma=False
    )
```

```python
import jax
import jax.numpy as jnp
from jax import lax
from jax.experimental import pallas as pl
from jax.experimental.pallas import tpu as pltpu
from jax.sharding import PartitionSpec as P

NF = 49152
EARLY = 8
GROUP = 8
CHUNKS = (56, 48)
BULK = 2**31
HIGHEST = lax.Precision.HIGHEST
VMEM_BYTES = 56 * 1024 * 1024


def pack_tiles(order, child_tiles, mask_columns, first, count, meta=None):
    tile_rows, tile_cols = child_tiles.shape[1:]
    stripes = tile_rows // 2
    base = first // GROUP
    extra = 0 if meta is None else meta.shape[0]
    width = 2 * GROUP + extra

    def body(order_ref, *refs):
        tiles, mask_ref = refs[:GROUP], refs[GROUP]
        out_ref, rows_ref = refs[-2], refs[-1]
        for i in range(GROUP):
            for s in range(2):
                rows = tiles[i][0, s * stripes : (s + 1) * stripes, :]
                column = mask_ref[0, s * stripes : (s + 1) * stripes, i : i + 1]
                rows_ref[pl.ds(2 * i + s, stripes, stride=2 * GROUP), :] = rows * column
        out_ref[:, : 2 * GROUP, :] = rows_ref[...].reshape(stripes, 2 * GROUP, tile_cols)
        if extra:
            meta_ref = refs[GROUP + 1]
            out_ref[:, 2 * GROUP :, :] = jnp.broadcast_to(
                meta_ref[...][None], (stripes, extra, tile_cols)
            )

    def tile_spec(i):
        return pl.BlockSpec(
            (1, tile_rows, tile_cols), lambda g, order_ref: (order_ref[first + g * GROUP + i], 0, 0)
        )

    in_specs = [tile_spec(i) for i in range(GROUP)]
    in_specs.append(pl.BlockSpec((1, tile_rows, GROUP), lambda g, order_ref: (base + g, 0, 0)))
    operands = [child_tiles] * GROUP + [mask_columns]
    if extra:
        in_specs.append(pl.BlockSpec((extra, tile_cols), lambda g, order_ref: (0, 0)))
        operands.append(meta)
    steps = count // GROUP
    return pl.pallas_call(
        body,
        grid_spec=pltpu.PrefetchScalarGridSpec(
            num_scalar_prefetch=1,
            grid=(steps,),
            in_specs=in_specs,
            out_specs=pl.BlockSpec((stripes, width, tile_cols), lambda g, order_ref: (0, g, 0)),
            scratch_shapes=[pltpu.VMEM((stripes * 2 * GROUP, tile_cols), jnp.float32)],
        ),
        out_shape=jax.ShapeDtypeStruct((stripes, steps * width, tile_cols), jnp.float32),
        compiler_params=pltpu.CompilerParams(vmem_limit_bytes=VMEM_BYTES),
        name="pack_tiles",
    )(order, *operands)


def add_pieces(targets, pieces, early, sums, first, weight):
    sources, count, two, lanes = pieces.shape
    n_sums = 6144
    per_step = 8
    fresh = sums is None

    def body(target_ref, pieces_ref, *refs):
        sums_ref = refs[-1]
        step = pl.program_id(0)

        @pl.when(step == 0)
        def _():
            sums_ref[...] = jnp.zeros_like(sums_ref) if fresh else refs[0][...]

        for n in range(per_step):
            source = step * per_step + n
            if fresh:
                for i in range(EARLY):
                    d = target_ref[source, i]
                    sums_ref[d] = sums_ref[d] + refs[0][n, i]
            for at in range(0, count, GROUP):
                ds = [target_ref[source, first + at + i] for i in range(GROUP)]
                news = [sums_ref[ds[i]] + pieces_ref[n, at + i] for i in range(GROUP)]
                for i in range(GROUP):
                    sums_ref[ds[i]] = news[i]

    def streamed(x):
        return pl.BlockSpec((per_step,) + x.shape[1:], lambda g, target_ref: (g, 0, 0, 0))

    whole = pl.BlockSpec(
        (n_sums, two, lanes), lambda g, target_ref: (0, 0, 0), pipeline_mode=pl.Buffered(1)
    )
    return pl.pallas_call(
        body,
        grid_spec=pltpu.PrefetchScalarGridSpec(
            num_scalar_prefetch=1,
            grid=(sources // per_step,),
            in_specs=[streamed(pieces), streamed(early) if fresh else whole],
            out_specs=whole,
        ),
        out_shape=jax.ShapeDtypeStruct((n_sums, two, lanes), jnp.float32),
        compiler_params=pltpu.CompilerParams(vmem_limit_bytes=VMEM_BYTES),
        cost_estimate=pl.CostEstimate(flops=weight, transcendentals=0, bytes_accessed=weight),
        name="add_pieces",
    )(targets, pieces, early if fresh else sums)


def add_top(spots, pieces, n_sums):
    sources, pitch, two, lanes = pieces.shape
    slots = spots.shape[1]

    def body(spot_ref, pieces_ref, out_ref, *parts):
        for part in parts:
            part[...] = jnp.zeros_like(part)

        def one(source, _):
            for i in range(slots):
                d = spot_ref[source, i]
                parts[i][d] = parts[i][d] + pieces_ref[source, i]
            return 0

        lax.fori_loop(0, sources, one, 0, unroll=4)
        total = parts[0][:n_sums]
        for part in parts[1:]:
            total = total + part[:n_sums]
        out_ref[...] = total

    return pl.pallas_call(
        body,
        grid_spec=pltpu.PrefetchScalarGridSpec(
            num_scalar_prefetch=1,
            grid=(1,),
            in_specs=[pl.BlockSpec(pieces.shape, lambda g, spot_ref: (0, 0, 0, 0))],
            out_specs=pl.BlockSpec((n_sums, two, lanes), lambda g, spot_ref: (0, 0, 0)),
            scratch_shapes=[pltpu.VMEM((n_sums + 8, two, lanes), jnp.float32)] * slots,
        ),
        out_shape=jax.ShapeDtypeStruct((n_sums, two, lanes), jnp.float32),
        compiler_params=pltpu.CompilerParams(vmem_limit_bytes=VMEM_BYTES),
        name="add_top",
    )(spots, pieces)


def factor_corner(corner, diagonal):
    size = corner.shape[2]
    n = 4

    def dot(a, b, transposed):
        dims = (((1,), (1 if transposed else 0,)), ((), ()))
        return lax.dot_general(a, b, dims, precision=HIGHEST, preferred_element_type=jnp.float32)

    def eliminate(block):
        groups = [block[8 * g : 8 * g + 8, :] for g in range(size // 8)]
        lane = lax.broadcasted_iota(jnp.int32, (8, size), 1)
        sub = lax.broadcasted_iota(jnp.int32, (8, size), 0)
        for p in range(size // 8):
            j0 = 8 * p
            rows = [jnp.broadcast_to(groups[p][r : r + 1, :], (8, size)) for r in range(8)]
            entry = [
                [
                    jnp.broadcast_to(rows[r][:, j0 + c : j0 + c + 1], (8, size)) if c >= r else None
                    for c in range(8)
                ]
                for r in range(8)
            ]
            ratio = [[None] * 8 for _ in range(8)]
            scaled = []
            done = groups[p]
            for r in range(8):
                row = jnp.where(jnp.logical_and(lane >= j0, lane < j0 + r), 0.0, rows[r])
                for q in range(r):
                    settled = jnp.logical_and(lane > j0 + q, lane < j0 + r)
                    row = row - ratio[r][q] * jnp.where(settled, 0.0, rows[q])
                done = jnp.where(sub == r, row, done)
                rows[r] = jnp.where(lane == j0 + r, 1.0, row)
                inverse = 1.0 / entry[r][r]
                settled = jnp.logical_and(lane > j0 + r, lane < j0 + 8)
                scaled.append(jnp.where(settled, 0.0, rows[r]) * inverse)
                for c in range(r + 1, 8):
                    ratio[c][r] = entry[r][c] * inverse
                for c in range(r + 1, 8):
                    for d in range(c, 8):
                        entry[c][d] = entry[c][d] - ratio[c][r] * entry[r][d]
            groups[p] = done
            inside = jnp.logical_and(lane >= j0, lane < j0 + 8)
            for g in range(p + 1, size // 8):
                columns = []
                result = jnp.where(inside, 0.0, groups[g])
                for c in range(8):
                    column = jnp.broadcast_to(groups[g][:, j0 + c : j0 + c + 1], (8, size))
                    for q in range(c):
                        column = column - ratio[c][q] * columns[q]
                    columns.append(column)
                    result = result - column * scaled[c]
                groups[g] = result
        return jnp.concatenate(groups, axis=0)

    def body(corner_ref, diag_ref, lower_ref, inverse_ref, flat_ref, a_ref, l_ref, i_ref):
        row = lax.broadcasted_iota(jnp.int32, (size, size), 0)
        col = lax.broadcasted_iota(jnp.int32, (size, size), 1)
        flat_ref[...] = corner_ref[...].reshape(size * 16, size)

        def raw(q, t):
            block = flat_ref[pl.ds(t * 4 + q, size, stride=16), :]
            if q == t:
                block = block + jnp.where(row == col, diag_ref[t : t + 1, :], 0.0)
            return block

        for q in range(n):
            for t in range(q + 1):
                block = raw(q, t)
                if q // 2 == t // 2:
                    block = 0.5 * (block + raw(t, q).T)
                a_ref[q * n + t] = block

        def step(k, _):
            done = eliminate(a_ref[k * n + k])
            pivots = jnp.sum(jnp.where(row == col, done, 0.0), axis=1, keepdims=True)
            root = jnp.sqrt(pivots)
            upper = jnp.where(col >= row, done, 0.0) / root
            inv = jnp.where(col < row, done, jnp.where(col == row, 1.0, 0.0)) / root
            l_ref[k * n + k] = upper.T
            i_ref[k * n + k] = inv
            for i in range(1, n):

                @pl.when(i > k)
                def _():
                    l_ref[i * n + k] = dot(a_ref[i * n + k], inv, True)

            for i in range(1, n):
                for j in range(1, i + 1):

                    @pl.when(j > k)
                    def _():
                        a_ref[i * n + j] = a_ref[i * n + j] - dot(
                            l_ref[i * n + k], l_ref[j * n + k], True
                        )

            return 0

        lax.fori_loop(0, n, step, 0)
        for i in range(n):
            for j in range(i):
                total = dot(l_ref[i * n + j], i_ref[j * n + j], False)
                for k in range(j + 1, i):
                    total = total + dot(l_ref[i * n + k], i_ref[k * n + j], False)
                i_ref[i * n + j] = -dot(i_ref[i * n + i], total, False)
        zero = jnp.zeros((size, size), jnp.float32)
        for i in range(n):
            for j in range(n):
                rows, cols = slice(i * size, (i + 1) * size), slice(j * size, (j + 1) * size)
                lower_ref[rows, cols] = l_ref[i * n + j] if j <= i else zero
                inverse_ref[rows, cols] = i_ref[i * n + j] if j <= i else zero

    shape = jax.ShapeDtypeStruct((n * size, n * size), jnp.float32)
    blocks = pltpu.VMEM((n * n, size, size), jnp.float32)
    return pl.pallas_call(
        body,
        out_shape=(shape, shape),
        scratch_shapes=[pltpu.VMEM((size * 16, size), jnp.float32), blocks, blocks, blocks],
        compiler_params=pltpu.CompilerParams(vmem_limit_bytes=VMEM_BYTES),
        name="factor_corner",
    )(corner, diagonal)


def update_rows(sums, top, inverse, own_rows, diagonal):
    blocks, n_col, halves, n_rows, lanes = sums.shape
    stripes, top_cols, _, _ = top.shape
    near = top_cols * lanes
    n_row = stripes // n_col
    share = n_rows // 2 // n_row
    pair = 8 // (blocks * halves)

    def dot(a, b, transposed):
        dims = (((1,), (1 if transposed else 0,)), ((), ()))
        return lax.dot_general(a, b, dims, precision=HIGHEST, preferred_element_type=jnp.float32)

    def body(
        sums_ref,
        panel_in_ref,
        top_ref,
        inverse_ref,
        own_ref,
        diag_ref,
        out_ref,
        panel_ref,
        factor_ref,
        flat_ref,
        result_ref,
        mixed_ref,
    ):
        g = pl.program_id(0)
        n_diag = diag_ref.shape[0]
        row = lax.broadcasted_iota(jnp.int32, (n_diag, lanes), 0)

        def with_diagonal(x, t):
            head = x[:n_diag] + jnp.where(row == t, diag_ref[...], 0.0)
            return jnp.concatenate([head, x[n_diag:]], axis=0)

        @pl.when(g == 0)
        def _():
            x = jnp.concatenate(
                [with_diagonal(panel_in_ref[0, t // 2, t % 2], t) for t in range(top_cols)], axis=1
            )
            panel = dot(x, inverse_ref[...], True)
            at = lax.broadcasted_iota(jnp.int32, (8, near), 0)
            head = jnp.where(at < 4, own_ref[...], panel[:8])
            panel = jnp.concatenate([head, panel[8:]], axis=0)
            panel_ref[...] = panel
            factor_ref[...] = dot(panel, inverse_ref[...], False)

        flat_ref[...] = top_ref[...].reshape(stripes * top_cols * 8, lanes)
        for i in range(pair):
            c = g * pair + i
            for cb in range(blocks):
                weights = jnp.concatenate(
                    [
                        jnp.concatenate(
                            [
                                flat_ref[
                                    pl.ds(
                                        k * 8 + (i * blocks + cb) * halves + h,
                                        stripes,
                                        stride=top_cols * 8,
                                    ),
                                    :,
                                ]
                                for k in range(top_cols)
                            ],
                            axis=1,
                        )
                        for h in range(halves)
                    ],
                    axis=0,
                )
                product = dot(factor_ref[...], weights, True)
                for h in range(halves):
                    t = (cb * n_col + c) * halves + h
                    result = with_diagonal(sums_ref[cb, i, h], t)
                    result = result - product[:, h * lanes : (h + 1) * lanes]
                    if cb == 0:
                        at = (i * halves + h) * lanes
                        result = jnp.where(g == 0, panel_ref[:, at : at + lanes], result)
                    result_ref[...] = result
                    for s in range(2):
                        mixed_ref[pl.ds(s * 4 + h * 2 + cb, n_rows // 2, stride=8), :] = result_ref[
                            pl.ds(s, n_rows // 2, stride=2), :
                        ]
            out_ref[:, i] = mixed_ref[...].reshape(n_row, share * 8, lanes)

    def fixed(*shape):
        return pl.BlockSpec(shape, lambda g: (0,) * len(shape))

    return pl.pallas_call(
        body,
        grid=(n_col // pair,),
        in_specs=[
            pl.BlockSpec((blocks, pair, halves, n_rows, lanes), lambda g: (0, g, 0, 0, 0)),
            pl.BlockSpec((1, 2, halves, n_rows, lanes), lambda g: (0, 0, 0, 0, 0)),
            pl.BlockSpec((stripes, top_cols, 8, lanes), lambda g: (0, 0, g, 0)),
            fixed(near, near),
            fixed(8, near),
            fixed(*diagonal.shape),
        ],
        out_specs=pl.BlockSpec((n_row, pair, share * 8, lanes), lambda g: (0, g, 0, 0)),
        out_shape=jax.ShapeDtypeStruct((n_row, n_col, share * 8, lanes), jnp.float32),
        scratch_shapes=[
            pltpu.VMEM((n_rows, near), jnp.float32),
            pltpu.VMEM((n_rows, near), jnp.float32),
            pltpu.VMEM((stripes * top_cols * 8, lanes), jnp.float32),
            pltpu.VMEM((n_rows, lanes), jnp.float32),
            pltpu.VMEM((n_rows * 4, lanes), jnp.float32),
        ],
        compiler_params=pltpu.CompilerParams(vmem_limit_bytes=VMEM_BYTES),
        name="update_rows",
    )(sums, sums, top, inverse, own_rows, diagonal)


def place_rows(received):
    stripes, width, lanes = received.shape
    units = width // 4

    def body(in_ref, out_ref):
        for s in range(2):
            out_ref[s] = in_ref[:, s]

    return pl.pallas_call(
        body,
        grid=(units // 2,),
        in_specs=[pl.BlockSpec((stripes, 2, 4, lanes), lambda g: (0, g, 0, 0))],
        out_specs=pl.BlockSpec((2, stripes, 4, lanes), lambda g: (g, 0, 0, 0)),
        out_shape=jax.ShapeDtypeStruct((units, stripes, 4, lanes), jnp.float32),
        compiler_params=pltpu.CompilerParams(vmem_limit_bytes=VMEM_BYTES),
        name="place_rows",
    )(received.reshape(stripes, units, 4, lanes))


def tile_order(tile_dest, col_tiles, top_rows, top_cols):
    total = tile_dest.shape[0]
    ids = jnp.arange(total, dtype=jnp.int32)
    same = tile_dest[:, None] == tile_dest[None, :]
    first_of = jnp.min(jnp.where(same, ids[None, :], total), axis=1)
    later = jnp.any(jnp.logical_and(same, ids[None, :] > ids[:, None]), axis=1)
    top = jnp.logical_and(tile_dest // col_tiles < top_rows, tile_dest % col_tiles < top_cols)
    rest = jnp.where(
        first_of < ids, 3 * total + first_of, jnp.where(later, total + ids, 2 * total + ids)
    )
    key = jnp.where(top, ids, rest)
    position = jnp.sum((key[None, :] < key[:, None]).astype(jnp.int32), axis=1)
    return (position[:, None] == ids[None, :]).astype(jnp.int32)


def on_device(child_tiles, tile_dest, tile_mask, tile_count, front_diagonal):
    axes = ("row", "col")
    n_row = lax.axis_size("row")
    n_col = lax.axis_size("col")
    devices = n_row * n_col
    me = lax.axis_index("row") * n_col + lax.axis_index("col")
    tile_total, tile_rows, lanes = child_tiles.shape
    col_blocks, panel = front_diagonal.shape
    halves = panel // lanes
    row_tiles = NF // tile_rows
    col_tiles = col_blocks * n_col * halves
    width = col_tiles * lanes
    top_rows = width // tile_rows
    top_cols = 2 * halves

    placed = tile_order(tile_dest, col_tiles, top_rows, top_cols)
    ids = jnp.arange(tile_total, dtype=jnp.int32)
    target = (tile_dest % col_tiles) * row_tiles + tile_dest // col_tiles
    order = jnp.sum(placed * ids[:, None], axis=0)
    target_sent = jnp.sum(placed * target[:, None], axis=0)
    live = (ids < tile_count[0]).astype(jnp.float32)
    mask_columns = lax.dot_general(
        tile_mask.astype(jnp.float32),
        placed.astype(jnp.float32) * live[:, None],
        (((0,), (0,)), ((), ())),
    )
    mask_columns = mask_columns.reshape(tile_rows, tile_total // GROUP, GROUP).transpose(1, 0, 2)
    meta = jnp.concatenate(
        [
            jnp.pad(target_sent.astype(jnp.float32), (0, lanes - tile_total))[None],
            front_diagonal.reshape(col_blocks * halves, lanes),
            jnp.zeros((8 - 1 - col_blocks * halves, lanes), jnp.float32),
        ],
        axis=0,
    )

    def exchange(x):
        return lax.all_to_all(x, axes, split_axis=0, concat_axis=0, tiled=True)

    early = exchange(pack_tiles(order, child_tiles, mask_columns, 0, EARLY, meta))
    at = EARLY
    first_pack = pack_tiles(order, child_tiles, mask_columns, at, CHUNKS[0])
    early, first_pack = lax.optimization_barrier((early, first_pack))
    received0 = exchange(first_pack)

    targets = early[:, 2 * EARLY, :].astype(jnp.int32)
    diagonal = early[:n_col, 2 * EARLY + 1 : 2 * EARLY + 1 + col_blocks * halves, :]
    diagonal = diagonal.reshape(n_col, col_blocks, panel).transpose(1, 0, 2)
    diagonal = diagonal.reshape(col_tiles, lanes)
    early = early.reshape(devices, EARLY + 4, 2, lanes)
    n_top = top_cols * top_rows
    tile, row = targets[:, :EARLY] // row_tiles, targets[:, :EARLY] % row_tiles
    spots = tile * top_rows + row % n_col * col_blocks + row // n_col
    spots = jnp.where(jnp.logical_and(tile < top_cols, row < top_rows), spots, n_top)
    view = add_top(spots, early, n_top)
    share = lax.all_gather(view.reshape(top_cols, 2 * top_rows, lanes), "row")

    second_pack = pack_tiles(order, child_tiles, mask_columns, at + CHUNKS[0], CHUNKS[1])
    received0, second_pack, share = lax.optimization_barrier((received0, second_pack, share))
    chips = n_col // 2
    my_chip, my_core = lax.axis_index("col") // 2, lax.axis_index("col") % 2
    half_top = jnp.zeros((n_row, chips) + share.shape[1:], jnp.float32)
    for step in range(chips):
        moved = share
        if step:
            hops = [(2 * i + k, 2 * ((i + step) % chips) + k) for i in range(chips) for k in range(2)]
            moved = lax.ppermute(share, "col", hops)
        origin = (my_chip + chips - step) % chips
        half_top = lax.dynamic_update_slice(half_top, moved[:, None], (0, origin, 0, 0, 0))
    received1 = exchange(second_pack)
    pieces = received0.reshape(devices, CHUNKS[0], 2, lanes)
    sums = add_pieces(targets, pieces, early, None, at, BULK)
    half_top, sums = lax.optimization_barrier((half_top, sums))
    other_top = lax.ppermute(half_top, "col", [(i, i + 1 - 2 * (i % 2)) for i in range(n_col)])
    top = jnp.where(
        my_core == jnp.arange(2).reshape(1, 1, 2, 1, 1, 1), half_top[:, :, None], other_top[:, :, None]
    )
    top = top.reshape(devices, top_cols, 2 * top_rows, lanes)
    corner = top.reshape(devices, top_cols, n_col, col_blocks, 2, lanes)[:, :, :2, 0]
    lower, inverse = factor_corner(corner.reshape(devices, 4 * top_cols, lanes), diagonal[:8])
    own_rows = lax.dynamic_slice(
        lower.reshape(top_cols, devices, top_cols * lanes),
        (0, me, 0),
        (top_cols, 1, top_cols * lanes),
    )
    own_rows = jnp.pad(own_rows.reshape(top_cols, top_cols * lanes), ((0, 8 - top_cols), (0, 0)))
    received1, inverse, own_rows = lax.optimization_barrier((received1, inverse, own_rows))
    pieces = received1.reshape(devices, CHUNKS[1], 2, lanes)
    sums = add_pieces(targets, pieces, None, sums, at + CHUNKS[0], BULK)

    own = jnp.where(jnp.arange(lanes, dtype=jnp.int32)[None, :] == me, diagonal, 0.0)
    result = update_rows(
        sums.reshape(col_blocks, n_col, halves, 2 * row_tiles, lanes), top, inverse, own_rows, own
    )
    received = exchange(result.reshape(devices, -1, lanes))
    rows = place_rows(received)
    rows = rows.reshape(NF // n_row, halves, col_blocks, lanes).transpose(0, 2, 1, 3)
    return rows.reshape(NF // n_row, col_blocks, panel)


def solution(mesh):
    in_specs = (
        P(("row", "col"), None, None),
        P(("row", "col")),
        P(("row", "col"), None),
        P(("row", "col")),
        P(None, "col"),
    )
    out_specs = P("row", None, "col")
    return jax.shard_map(
        on_device, mesh=mesh, in_specs=in_specs, out_specs=out_specs, check_vma=False
    )
```

```python
import jax
import jax.numpy as jnp
from jax import lax
from jax.experimental import pallas as pl
from jax.experimental.pallas import tpu as pltpu
from jax.sharding import PartitionSpec as P

NF = 49152
EARLY = 8
GROUP = 8
CHUNKS = (56, 48)
BULK = 2**31
HIGHEST = lax.Precision.HIGHEST
VMEM_BYTES = 56 * 1024 * 1024


def pack_tiles(order, child_tiles, mask_columns, first, count, meta=None):
    tile_rows, tile_cols = child_tiles.shape[1:]
    stripes = tile_rows // 2
    base = first // GROUP
    extra = 0 if meta is None else meta.shape[0]
    width = 2 * GROUP + extra

    def body(order_ref, *refs):
        tiles, mask_ref = refs[:GROUP], refs[GROUP]
        out_ref, rows_ref = refs[-2], refs[-1]
        for i in range(GROUP):
            for s in range(2):
                rows = tiles[i][0, s * stripes : (s + 1) * stripes, :]
                column = mask_ref[0, s * stripes : (s + 1) * stripes, i : i + 1]
                rows_ref[pl.ds(2 * i + s, stripes, stride=2 * GROUP), :] = rows * column
        out_ref[:, : 2 * GROUP, :] = rows_ref[...].reshape(stripes, 2 * GROUP, tile_cols)
        if extra:
            meta_ref = refs[GROUP + 1]
            out_ref[:, 2 * GROUP :, :] = jnp.broadcast_to(
                meta_ref[...][None], (stripes, extra, tile_cols)
            )

    def tile_spec(i):
        return pl.BlockSpec(
            (1, tile_rows, tile_cols), lambda g, order_ref: (order_ref[first + g * GROUP + i], 0, 0)
        )

    in_specs = [tile_spec(i) for i in range(GROUP)]
    in_specs.append(pl.BlockSpec((1, tile_rows, GROUP), lambda g, order_ref: (base + g, 0, 0)))
    operands = [child_tiles] * GROUP + [mask_columns]
    if extra:
        in_specs.append(pl.BlockSpec((extra, tile_cols), lambda g, order_ref: (0, 0)))
        operands.append(meta)
    steps = count // GROUP
    return pl.pallas_call(
        body,
        grid_spec=pltpu.PrefetchScalarGridSpec(
            num_scalar_prefetch=1,
            grid=(steps,),
            in_specs=in_specs,
            out_specs=pl.BlockSpec((stripes, width, tile_cols), lambda g, order_ref: (0, g, 0)),
            scratch_shapes=[pltpu.VMEM((stripes * 2 * GROUP, tile_cols), jnp.float32)],
        ),
        out_shape=jax.ShapeDtypeStruct((stripes, steps * width, tile_cols), jnp.float32),
        compiler_params=pltpu.CompilerParams(vmem_limit_bytes=VMEM_BYTES),
        name="pack_tiles",
    )(order, *operands)


def add_pieces(targets, pieces, early, sums, first, weight):
    sources, count, two, lanes = pieces.shape
    n_sums = 6144
    per_step = 8
    fresh = sums is None

    def body(target_ref, pieces_ref, *refs):
        sums_ref = refs[-1]
        step = pl.program_id(0)

        @pl.when(step == 0)
        def _():
            sums_ref[...] = jnp.zeros_like(sums_ref) if fresh else refs[0][...]

        for n in range(per_step):
            source = step * per_step + n
            if fresh:
                for i in range(EARLY):
                    d = target_ref[source, i]
                    sums_ref[d] = sums_ref[d] + refs[0][n, i]
            for at in range(0, count, GROUP):
                ds = [target_ref[source, first + at + i] for i in range(GROUP)]
                news = [sums_ref[ds[i]] + pieces_ref[n, at + i] for i in range(GROUP)]
                for i in range(GROUP):
                    sums_ref[ds[i]] = news[i]

    def streamed(x):
        return pl.BlockSpec((per_step,) + x.shape[1:], lambda g, target_ref: (g, 0, 0, 0))

    whole = pl.BlockSpec(
        (n_sums, two, lanes), lambda g, target_ref: (0, 0, 0), pipeline_mode=pl.Buffered(1)
    )
    return pl.pallas_call(
        body,
        grid_spec=pltpu.PrefetchScalarGridSpec(
            num_scalar_prefetch=1,
            grid=(sources // per_step,),
            in_specs=[streamed(pieces), streamed(early) if fresh else whole],
            out_specs=whole,
        ),
        out_shape=jax.ShapeDtypeStruct((n_sums, two, lanes), jnp.float32),
        compiler_params=pltpu.CompilerParams(vmem_limit_bytes=VMEM_BYTES),
        cost_estimate=pl.CostEstimate(flops=weight, transcendentals=0, bytes_accessed=weight),
        name="add_pieces",
    )(targets, pieces, early if fresh else sums)


def add_top(spots, pieces, n_sums):
    sources, pitch, two, lanes = pieces.shape
    slots = spots.shape[1]

    def body(spot_ref, pieces_ref, out_ref, *parts):
        for part in parts:
            part[...] = jnp.zeros_like(part)

        def one(source, _):
            for i in range(slots):
                d = spot_ref[source, i]
                parts[i][d] = parts[i][d] + pieces_ref[source, i]
            return 0

        lax.fori_loop(0, sources, one, 0, unroll=4)
        total = parts[0][:n_sums]
        for part in parts[1:]:
            total = total + part[:n_sums]
        out_ref[...] = total

    return pl.pallas_call(
        body,
        grid_spec=pltpu.PrefetchScalarGridSpec(
            num_scalar_prefetch=1,
            grid=(1,),
            in_specs=[pl.BlockSpec(pieces.shape, lambda g, spot_ref: (0, 0, 0, 0))],
            out_specs=pl.BlockSpec((n_sums, two, lanes), lambda g, spot_ref: (0, 0, 0)),
            scratch_shapes=[pltpu.VMEM((n_sums + 8, two, lanes), jnp.float32)] * slots,
        ),
        out_shape=jax.ShapeDtypeStruct((n_sums, two, lanes), jnp.float32),
        compiler_params=pltpu.CompilerParams(vmem_limit_bytes=VMEM_BYTES),
        name="add_top",
    )(spots, pieces)


def factor_corner(corner, diagonal):
    size = corner.shape[2]
    n = 4

    def dot(a, b, transposed):
        dims = (((1,), (1 if transposed else 0,)), ((), ()))
        return lax.dot_general(a, b, dims, precision=HIGHEST, preferred_element_type=jnp.float32)

    def eliminate(block):
        groups = [block[8 * g : 8 * g + 8, :] for g in range(size // 8)]
        lane = lax.broadcasted_iota(jnp.int32, (8, size), 1)
        sub = lax.broadcasted_iota(jnp.int32, (8, size), 0)
        for p in range(size // 8):
            j0 = 8 * p
            rows = [jnp.broadcast_to(groups[p][r : r + 1, :], (8, size)) for r in range(8)]
            entry = [
                [
                    jnp.broadcast_to(rows[r][:, j0 + c : j0 + c + 1], (8, size)) if c >= r else None
                    for c in range(8)
                ]
                for r in range(8)
            ]
            ratio = [[None] * 8 for _ in range(8)]
            scaled = []
            done = groups[p]
            for r in range(8):
                row = jnp.where(jnp.logical_and(lane >= j0, lane < j0 + r), 0.0, rows[r])
                for q in range(r):
                    settled = jnp.logical_and(lane > j0 + q, lane < j0 + r)
                    row = row - ratio[r][q] * jnp.where(settled, 0.0, rows[q])
                done = jnp.where(sub == r, row, done)
                rows[r] = jnp.where(lane == j0 + r, 1.0, row)
                inverse = 1.0 / entry[r][r]
                settled = jnp.logical_and(lane > j0 + r, lane < j0 + 8)
                scaled.append(jnp.where(settled, 0.0, rows[r]) * inverse)
                for c in range(r + 1, 8):
                    ratio[c][r] = entry[r][c] * inverse
                for c in range(r + 1, 8):
                    for d in range(c, 8):
                        entry[c][d] = entry[c][d] - ratio[c][r] * entry[r][d]
            groups[p] = done
            inside = jnp.logical_and(lane >= j0, lane < j0 + 8)
            for g in range(p + 1, size // 8):
                columns = []
                result = jnp.where(inside, 0.0, groups[g])
                for c in range(8):
                    column = jnp.broadcast_to(groups[g][:, j0 + c : j0 + c + 1], (8, size))
                    for q in range(c):
                        column = column - ratio[c][q] * columns[q]
                    columns.append(column)
                    result = result - column * scaled[c]
                groups[g] = result
        return jnp.concatenate(groups, axis=0)

    def body(corner_ref, diag_ref, lower_ref, inverse_ref, flat_ref, a_ref, l_ref, i_ref):
        row = lax.broadcasted_iota(jnp.int32, (size, size), 0)
        col = lax.broadcasted_iota(jnp.int32, (size, size), 1)
        flat_ref[...] = corner_ref[...].reshape(size * 16, size)

        def raw(q, t):
            block = flat_ref[pl.ds(t * 4 + q, size, stride=16), :]
            if q == t:
                block = block + jnp.where(row == col, diag_ref[t : t + 1, :], 0.0)
            return block

        for q in range(n):
            for t in range(q + 1):
                block = raw(q, t)
                if q // 2 == t // 2:
                    block = 0.5 * (block + raw(t, q).T)
                a_ref[q * n + t] = block

        def step(k, _):
            done = eliminate(a_ref[k * n + k])
            pivots = jnp.sum(jnp.where(row == col, done, 0.0), axis=1, keepdims=True)
            root = jnp.sqrt(pivots)
            upper = jnp.where(col >= row, done, 0.0) / root
            inv = jnp.where(col < row, done, jnp.where(col == row, 1.0, 0.0)) / root
            l_ref[k * n + k] = upper.T
            i_ref[k * n + k] = inv
            for i in range(1, n):

                @pl.when(i > k)
                def _():
                    l_ref[i * n + k] = dot(a_ref[i * n + k], inv, True)

            for i in range(1, n):
                for j in range(1, i + 1):

                    @pl.when(j > k)
                    def _():
                        a_ref[i * n + j] = a_ref[i * n + j] - dot(
                            l_ref[i * n + k], l_ref[j * n + k], True
                        )

            return 0

        lax.fori_loop(0, n, step, 0)
        for i in range(n):
            for j in range(i):
                total = dot(l_ref[i * n + j], i_ref[j * n + j], False)
                for k in range(j + 1, i):
                    total = total + dot(l_ref[i * n + k], i_ref[k * n + j], False)
                i_ref[i * n + j] = -dot(i_ref[i * n + i], total, False)
        zero = jnp.zeros((size, size), jnp.float32)
        for i in range(n):
            for j in range(n):
                rows, cols = slice(i * size, (i + 1) * size), slice(j * size, (j + 1) * size)
                lower_ref[rows, cols] = l_ref[i * n + j] if j <= i else zero
                inverse_ref[rows, cols] = i_ref[i * n + j] if j <= i else zero

    shape = jax.ShapeDtypeStruct((n * size, n * size), jnp.float32)
    blocks = pltpu.VMEM((n * n, size, size), jnp.float32)
    return pl.pallas_call(
        body,
        out_shape=(shape, shape),
        scratch_shapes=[pltpu.VMEM((size * 16, size), jnp.float32), blocks, blocks, blocks],
        compiler_params=pltpu.CompilerParams(vmem_limit_bytes=VMEM_BYTES),
        name="factor_corner",
    )(corner, diagonal)


def update_rows(core, sums, top, other_top, inverse, own_rows, diagonal):
    blocks, n_col, halves, n_rows, lanes = sums.shape
    pairs, top_cols, _, _ = top.shape
    stripes = 2 * pairs
    near = top_cols * lanes
    n_row = stripes // n_col
    share = n_rows // 2 // n_row
    pair = 8 // (blocks * halves)

    def dot(a, b, transposed):
        dims = (((1,), (1 if transposed else 0,)), ((), ()))
        return lax.dot_general(a, b, dims, precision=HIGHEST, preferred_element_type=jnp.float32)

    def body(
        core_ref,
        sums_ref,
        panel_in_ref,
        top_ref,
        other_ref,
        inverse_ref,
        own_ref,
        diag_ref,
        out_ref,
        panel_ref,
        factor_ref,
        flat_ref,
        result_ref,
        mixed_ref,
    ):
        g = pl.program_id(0)
        n_diag = diag_ref.shape[0]
        row = lax.broadcasted_iota(jnp.int32, (n_diag, lanes), 0)

        def with_diagonal(x, t):
            head = x[:n_diag] + jnp.where(row == t, diag_ref[...], 0.0)
            return jnp.concatenate([head, x[n_diag:]], axis=0)

        @pl.when(g == 0)
        def _():
            x = jnp.concatenate(
                [with_diagonal(panel_in_ref[0, t // 2, t % 2], t) for t in range(top_cols)], axis=1
            )
            panel = dot(x, inverse_ref[...], True)
            at = lax.broadcasted_iota(jnp.int32, (8, near), 0)
            head = jnp.where(at < 4, own_ref[...], panel[:8])
            panel = jnp.concatenate([head, panel[8:]], axis=0)
            panel_ref[...] = panel
            factor_ref[...] = dot(panel, inverse_ref[...], False)

        mine, theirs = top_ref[...], other_ref[...]
        first = core_ref[0] == 0
        both = [jnp.where(first, mine, theirs), jnp.where(first, theirs, mine)]
        both = [x.reshape(pairs, 1, top_cols * 8, lanes) for x in both]
        flat_ref[...] = jnp.concatenate(both, axis=1).reshape(stripes * top_cols * 8, lanes)
        for i in range(pair):
            c = g * pair + i
            for cb in range(blocks):
                weights = jnp.concatenate(
                    [
                        jnp.concatenate(
                            [
                                flat_ref[
                                    pl.ds(
                                        k * 8 + (i * blocks + cb) * halves + h,
                                        stripes,
                                        stride=top_cols * 8,
                                    ),
                                    :,
                                ]
                                for k in range(top_cols)
                            ],
                            axis=1,
                        )
                        for h in range(halves)
                    ],
                    axis=0,
                )
                product = dot(factor_ref[...], weights, True)
                for h in range(halves):
                    t = (cb * n_col + c) * halves + h
                    result = with_diagonal(sums_ref[cb, i, h], t)
                    result = result - product[:, h * lanes : (h + 1) * lanes]
                    if cb == 0:
                        at = (i * halves + h) * lanes
                        result = jnp.where(g == 0, panel_ref[:, at : at + lanes], result)
                    result_ref[...] = result
                    for s in range(2):
                        mixed_ref[pl.ds(s * 4 + h * 2 + cb, n_rows // 2, stride=8), :] = result_ref[
                            pl.ds(s, n_rows // 2, stride=2), :
                        ]
            out_ref[:, i] = mixed_ref[...].reshape(n_row, share * 8, lanes)

    def fixed(*shape):
        return pl.BlockSpec(shape, lambda g, core_ref: (0,) * len(shape))

    top_spec = pl.BlockSpec((pairs, top_cols, 8, lanes), lambda g, core_ref: (0, 0, g, 0))
    return pl.pallas_call(
        body,
        grid_spec=pltpu.PrefetchScalarGridSpec(
            num_scalar_prefetch=1,
            grid=(n_col // pair,),
            in_specs=[
                pl.BlockSpec(
                    (blocks, pair, halves, n_rows, lanes), lambda g, core_ref: (0, g, 0, 0, 0)
                ),
                pl.BlockSpec((1, 2, halves, n_rows, lanes), lambda g, core_ref: (0, 0, 0, 0, 0)),
                top_spec,
                top_spec,
                fixed(near, near),
                fixed(8, near),
                fixed(*diagonal.shape),
            ],
            out_specs=pl.BlockSpec(
                (n_row, pair, share * 8, lanes), lambda g, core_ref: (0, g, 0, 0)
            ),
            scratch_shapes=[
                pltpu.VMEM((n_rows, near), jnp.float32),
                pltpu.VMEM((n_rows, near), jnp.float32),
                pltpu.VMEM((stripes * top_cols * 8, lanes), jnp.float32),
                pltpu.VMEM((n_rows, lanes), jnp.float32),
                pltpu.VMEM((n_rows * 4, lanes), jnp.float32),
            ],
        ),
        out_shape=jax.ShapeDtypeStruct((n_row, n_col, share * 8, lanes), jnp.float32),
        compiler_params=pltpu.CompilerParams(vmem_limit_bytes=VMEM_BYTES),
        name="update_rows",
    )(core, sums, sums, top, other_top, inverse, own_rows, diagonal)


def place_rows(received):
    stripes, width, lanes = received.shape
    units = width // 4

    def body(in_ref, out_ref):
        for s in range(2):
            out_ref[s] = in_ref[:, s]

    return pl.pallas_call(
        body,
        grid=(units // 2,),
        in_specs=[pl.BlockSpec((stripes, 2, 4, lanes), lambda g: (0, g, 0, 0))],
        out_specs=pl.BlockSpec((2, stripes, 4, lanes), lambda g: (g, 0, 0, 0)),
        out_shape=jax.ShapeDtypeStruct((units, stripes, 4, lanes), jnp.float32),
        compiler_params=pltpu.CompilerParams(vmem_limit_bytes=VMEM_BYTES),
        name="place_rows",
    )(received.reshape(stripes, units, 4, lanes))


def tile_order(tile_dest, col_tiles, top_rows, top_cols):
    total = tile_dest.shape[0]
    ids = jnp.arange(total, dtype=jnp.int32)
    same = tile_dest[:, None] == tile_dest[None, :]
    first_of = jnp.min(jnp.where(same, ids[None, :], total), axis=1)
    later = jnp.any(jnp.logical_and(same, ids[None, :] > ids[:, None]), axis=1)
    top = jnp.logical_and(tile_dest // col_tiles < top_rows, tile_dest % col_tiles < top_cols)
    rest = jnp.where(
        first_of < ids, 3 * total + first_of, jnp.where(later, total + ids, 2 * total + ids)
    )
    key = jnp.where(top, ids, rest)
    position = jnp.sum((key[None, :] < key[:, None]).astype(jnp.int32), axis=1)
    return (position[:, None] == ids[None, :]).astype(jnp.int32)


def on_device(child_tiles, tile_dest, tile_mask, tile_count, front_diagonal):
    axes = ("row", "col")
    n_row = lax.axis_size("row")
    n_col = lax.axis_size("col")
    devices = n_row * n_col
    me = lax.axis_index("row") * n_col + lax.axis_index("col")
    tile_total, tile_rows, lanes = child_tiles.shape
    col_blocks, panel = front_diagonal.shape
    halves = panel // lanes
    row_tiles = NF // tile_rows
    col_tiles = col_blocks * n_col * halves
    width = col_tiles * lanes
    top_rows = width // tile_rows
    top_cols = 2 * halves

    placed = tile_order(tile_dest, col_tiles, top_rows, top_cols)
    ids = jnp.arange(tile_total, dtype=jnp.int32)
    target = (tile_dest % col_tiles) * row_tiles + tile_dest // col_tiles
    order = jnp.sum(placed * ids[:, None], axis=0)
    target_sent = jnp.sum(placed * target[:, None], axis=0)
    live = (ids < tile_count[0]).astype(jnp.float32)
    mask_columns = lax.dot_general(
        tile_mask.astype(jnp.float32),
        placed.astype(jnp.float32) * live[:, None],
        (((0,), (0,)), ((), ())),
    )
    mask_columns = mask_columns.reshape(tile_rows, tile_total // GROUP, GROUP).transpose(1, 0, 2)
    meta = jnp.concatenate(
        [
            jnp.pad(target_sent.astype(jnp.float32), (0, lanes - tile_total))[None],
            front_diagonal.reshape(col_blocks * halves, lanes),
            jnp.zeros((8 - 1 - col_blocks * halves, lanes), jnp.float32),
        ],
        axis=0,
    )

    def exchange(x):
        return lax.all_to_all(x, axes, split_axis=0, concat_axis=0, tiled=True)

    early = exchange(pack_tiles(order, child_tiles, mask_columns, 0, EARLY, meta))
    at = EARLY
    first_pack = pack_tiles(order, child_tiles, mask_columns, at, CHUNKS[0])
    early, first_pack = lax.optimization_barrier((early, first_pack))
    received0 = exchange(first_pack)

    targets = early[:, 2 * EARLY, :].astype(jnp.int32)
    diagonal = early[:n_col, 2 * EARLY + 1 : 2 * EARLY + 1 + col_blocks * halves, :]
    diagonal = diagonal.reshape(n_col, col_blocks, panel).transpose(1, 0, 2)
    diagonal = diagonal.reshape(col_tiles, lanes)
    early = early.reshape(devices, EARLY + 4, 2, lanes)
    n_top = top_cols * top_rows
    tile, row = targets[:, :EARLY] // row_tiles, targets[:, :EARLY] % row_tiles
    spots = tile * top_rows + row % n_col * col_blocks + row // n_col
    spots = jnp.where(jnp.logical_and(tile < top_cols, row < top_rows), spots, n_top)
    view = add_top(spots, early, n_top)
    view = view.reshape(top_cols, 2 * top_rows, lanes)
    chips = n_col // 2
    my_chip, my_core = lax.axis_index("col") // 2, lax.axis_index("col") % 2
    top = jnp.zeros((chips,) + view.shape, jnp.float32)
    for step in range(chips):
        moved = view
        if step:
            hops = [(2 * i + k, 2 * ((i + step) % chips) + k) for i in range(chips) for k in range(2)]
            moved = lax.ppermute(view, "col", hops)
        origin = (my_chip + chips - step) % chips
        top = lax.dynamic_update_slice(top, moved[None], (origin, 0, 0, 0))
    corner = top.reshape(chips, top_cols, n_col, col_blocks, 2, lanes)[:, :, :2, 0]
    corner = lax.all_gather(corner.reshape(chips, 4 * top_cols, lanes), "row")

    second_pack = pack_tiles(order, child_tiles, mask_columns, at + CHUNKS[0], CHUNKS[1])
    received0, second_pack, corner, top = lax.optimization_barrier(
        (received0, second_pack, corner, top)
    )

    def from_other_core(x):
        return lax.ppermute(x, "col", [(i, i + 1 - 2 * (i % 2)) for i in range(n_col)])

    top = lax.all_gather(top, "row").reshape(devices // 2, top_cols, 2 * top_rows, lanes)
    corner = corner.reshape(devices // 2, 1, 4 * top_cols, lanes)
    other = from_other_core(corner)
    corner = jnp.where(
        my_core == 0,
        jnp.concatenate([corner, other], axis=1),
        jnp.concatenate([other, corner], axis=1),
    )
    received1 = exchange(second_pack)
    pieces = received0.reshape(devices, CHUNKS[0], 2, lanes)
    sums = add_pieces(targets, pieces, early, None, at, BULK)
    corner, sums = lax.optimization_barrier((corner, sums))
    lower, inverse = factor_corner(corner.reshape(devices, 4 * top_cols, lanes), diagonal[:8])
    own_rows = lax.dynamic_slice(
        lower.reshape(top_cols, devices, top_cols * lanes),
        (0, me, 0),
        (top_cols, 1, top_cols * lanes),
    )
    own_rows = jnp.pad(own_rows.reshape(top_cols, top_cols * lanes), ((0, 8 - top_cols), (0, 0)))
    received1, inverse, own_rows, top = lax.optimization_barrier(
        (received1, inverse, own_rows, top)
    )
    other_top = from_other_core(top)
    pieces = received1.reshape(devices, CHUNKS[1], 2, lanes)
    sums = add_pieces(targets, pieces, None, sums, at + CHUNKS[0], BULK)

    own = jnp.where(jnp.arange(lanes, dtype=jnp.int32)[None, :] == me, diagonal, 0.0)
    result = update_rows(
        my_core.reshape(1),
        sums.reshape(col_blocks, n_col, halves, 2 * row_tiles, lanes), top, other_top, inverse, own_rows, own
    )
    received = exchange(result.reshape(devices, -1, lanes))
    rows = place_rows(received)
    rows = rows.reshape(NF // n_row, halves, col_blocks, lanes).transpose(0, 2, 1, 3)
    return rows.reshape(NF // n_row, col_blocks, panel)


def solution(mesh):
    in_specs = (
        P(("row", "col"), None, None),
        P(("row", "col")),
        P(("row", "col"), None),
        P(("row", "col")),
        P(None, "col"),
    )
    out_specs = P("row", None, "col")
    return jax.shard_map(
        on_device, mesh=mesh, in_specs=in_specs, out_specs=out_specs, check_vma=False
    )
```

```python
import jax
import jax.numpy as jnp
from jax import lax
from jax.experimental import pallas as pl
from jax.experimental.pallas import tpu as pltpu
from jax.sharding import PartitionSpec as P

NF = 49152
EARLY = 8
GROUP = 8
CHUNKS = (64, 40)
BULK = 2**31
HIGHEST = lax.Precision.HIGHEST
VMEM_BYTES = 56 * 1024 * 1024


def pack_tiles(order, child_tiles, mask_columns, first, count, meta=None):
    tile_rows, tile_cols = child_tiles.shape[1:]
    stripes = tile_rows // 2
    base = first // GROUP
    extra = 0 if meta is None else meta.shape[0]
    width = 2 * GROUP + extra

    def body(order_ref, *refs):
        tiles, mask_ref = refs[:GROUP], refs[GROUP]
        out_ref, rows_ref = refs[-2], refs[-1]
        for i in range(GROUP):
            for s in range(2):
                rows = tiles[i][0, s * stripes : (s + 1) * stripes, :]
                column = mask_ref[0, s * stripes : (s + 1) * stripes, i : i + 1]
                rows_ref[pl.ds(2 * i + s, stripes, stride=2 * GROUP), :] = rows * column
        out_ref[:, : 2 * GROUP, :] = rows_ref[...].reshape(stripes, 2 * GROUP, tile_cols)
        if extra:
            meta_ref = refs[GROUP + 1]
            out_ref[:, 2 * GROUP :, :] = jnp.broadcast_to(
                meta_ref[...][None], (stripes, extra, tile_cols)
            )

    def tile_spec(i):
        return pl.BlockSpec(
            (1, tile_rows, tile_cols), lambda g, order_ref: (order_ref[first + g * GROUP + i], 0, 0)
        )

    in_specs = [tile_spec(i) for i in range(GROUP)]
    in_specs.append(pl.BlockSpec((1, tile_rows, GROUP), lambda g, order_ref: (base + g, 0, 0)))
    operands = [child_tiles] * GROUP + [mask_columns]
    if extra:
        in_specs.append(pl.BlockSpec((extra, tile_cols), lambda g, order_ref: (0, 0)))
        operands.append(meta)
    steps = count // GROUP
    return pl.pallas_call(
        body,
        grid_spec=pltpu.PrefetchScalarGridSpec(
            num_scalar_prefetch=1,
            grid=(steps,),
            in_specs=in_specs,
            out_specs=pl.BlockSpec((stripes, width, tile_cols), lambda g, order_ref: (0, g, 0)),
            scratch_shapes=[pltpu.VMEM((stripes * 2 * GROUP, tile_cols), jnp.float32)],
        ),
        out_shape=jax.ShapeDtypeStruct((stripes, steps * width, tile_cols), jnp.float32),
        compiler_params=pltpu.CompilerParams(vmem_limit_bytes=VMEM_BYTES),
        name="pack_tiles",
    )(order, *operands)


def add_pieces(targets, pieces, early, sums, first, weight):
    sources, count, two, lanes = pieces.shape
    n_sums = 6144
    per_step = 8
    fresh = sums is None

    def body(target_ref, pieces_ref, *refs):
        sums_ref = refs[-1]
        step = pl.program_id(0)

        @pl.when(step == 0)
        def _():
            sums_ref[...] = jnp.zeros_like(sums_ref) if fresh else refs[0][...]

        for n in range(per_step):
            source = step * per_step + n
            if fresh:
                for i in range(EARLY):
                    d = target_ref[source, i]
                    sums_ref[d] = sums_ref[d] + refs[0][n, i]
            for at in range(0, count, GROUP):
                ds = [target_ref[source, first + at + i] for i in range(GROUP)]
                news = [sums_ref[ds[i]] + pieces_ref[n, at + i] for i in range(GROUP)]
                for i in range(GROUP):
                    sums_ref[ds[i]] = news[i]

    def streamed(x):
        return pl.BlockSpec((per_step,) + x.shape[1:], lambda g, target_ref: (g, 0, 0, 0))

    whole = pl.BlockSpec(
        (n_sums, two, lanes), lambda g, target_ref: (0, 0, 0), pipeline_mode=pl.Buffered(1)
    )
    return pl.pallas_call(
        body,
        grid_spec=pltpu.PrefetchScalarGridSpec(
            num_scalar_prefetch=1,
            grid=(sources // per_step,),
            in_specs=[streamed(pieces), streamed(early) if fresh else whole],
            out_specs=whole,
        ),
        out_shape=jax.ShapeDtypeStruct((n_sums, two, lanes), jnp.float32),
        compiler_params=pltpu.CompilerParams(vmem_limit_bytes=VMEM_BYTES),
        cost_estimate=pl.CostEstimate(flops=weight, transcendentals=0, bytes_accessed=weight),
        name="add_pieces",
    )(targets, pieces, early if fresh else sums)


def add_top(spots, pieces, n_sums):
    sources, pitch, two, lanes = pieces.shape
    slots = spots.shape[1]

    def body(spot_ref, pieces_ref, out_ref, *parts):
        for part in parts:
            part[...] = jnp.zeros_like(part)

        def one(source, _):
            for i in range(slots):
                d = spot_ref[source, i]
                parts[i][d] = parts[i][d] + pieces_ref[source, i]
            return 0

        lax.fori_loop(0, sources, one, 0, unroll=4)
        total = parts[0][:n_sums]
        for part in parts[1:]:
            total = total + part[:n_sums]
        out_ref[...] = total

    return pl.pallas_call(
        body,
        grid_spec=pltpu.PrefetchScalarGridSpec(
            num_scalar_prefetch=1,
            grid=(1,),
            in_specs=[pl.BlockSpec(pieces.shape, lambda g, spot_ref: (0, 0, 0, 0))],
            out_specs=pl.BlockSpec((n_sums, two, lanes), lambda g, spot_ref: (0, 0, 0)),
            scratch_shapes=[pltpu.VMEM((n_sums + 8, two, lanes), jnp.float32)] * slots,
        ),
        out_shape=jax.ShapeDtypeStruct((n_sums, two, lanes), jnp.float32),
        compiler_params=pltpu.CompilerParams(vmem_limit_bytes=VMEM_BYTES),
        name="add_top",
    )(spots, pieces)


def factor_corner(corner, diagonal):
    size = corner.shape[2]
    n = 4

    def dot(a, b, transposed):
        dims = (((1,), (1 if transposed else 0,)), ((), ()))
        return lax.dot_general(a, b, dims, precision=HIGHEST, preferred_element_type=jnp.float32)

    def eliminate(block):
        groups = [block[8 * g : 8 * g + 8, :] for g in range(size // 8)]
        lane = lax.broadcasted_iota(jnp.int32, (8, size), 1)
        sub = lax.broadcasted_iota(jnp.int32, (8, size), 0)
        for p in range(size // 8):
            j0 = 8 * p
            rows = [jnp.broadcast_to(groups[p][r : r + 1, :], (8, size)) for r in range(8)]
            entry = [
                [
                    jnp.broadcast_to(rows[r][:, j0 + c : j0 + c + 1], (8, size)) if c >= r else None
                    for c in range(8)
                ]
                for r in range(8)
            ]
            ratio = [[None] * 8 for _ in range(8)]
            scaled = []
            done = groups[p]
            for r in range(8):
                row = jnp.where(jnp.logical_and(lane >= j0, lane < j0 + r), 0.0, rows[r])
                for q in range(r):
                    settled = jnp.logical_and(lane > j0 + q, lane < j0 + r)
                    row = row - ratio[r][q] * jnp.where(settled, 0.0, rows[q])
                done = jnp.where(sub == r, row, done)
                rows[r] = jnp.where(lane == j0 + r, 1.0, row)
                inverse = 1.0 / entry[r][r]
                settled = jnp.logical_and(lane > j0 + r, lane < j0 + 8)
                scaled.append(jnp.where(settled, 0.0, rows[r]) * inverse)
                for c in range(r + 1, 8):
                    ratio[c][r] = entry[r][c] * inverse
                for c in range(r + 1, 8):
                    for d in range(c, 8):
                        entry[c][d] = entry[c][d] - ratio[c][r] * entry[r][d]
            groups[p] = done
            inside = jnp.logical_and(lane >= j0, lane < j0 + 8)
            for g in range(p + 1, size // 8):
                columns = []
                result = jnp.where(inside, 0.0, groups[g])
                for c in range(8):
                    column = jnp.broadcast_to(groups[g][:, j0 + c : j0 + c + 1], (8, size))
                    for q in range(c):
                        column = column - ratio[c][q] * columns[q]
                    columns.append(column)
                    result = result - column * scaled[c]
                groups[g] = result
        return jnp.concatenate(groups, axis=0)

    def body(corner_ref, diag_ref, lower_ref, inverse_ref, flat_ref, a_ref, l_ref, i_ref):
        row = lax.broadcasted_iota(jnp.int32, (size, size), 0)
        col = lax.broadcasted_iota(jnp.int32, (size, size), 1)
        flat_ref[...] = corner_ref[...].reshape(size * 16, size)

        def raw(q, t):
            block = flat_ref[pl.ds(t * 4 + q, size, stride=16), :]
            if q == t:
                block = block + jnp.where(row == col, diag_ref[t : t + 1, :], 0.0)
            return block

        for q in range(n):
            for t in range(q + 1):
                block = raw(q, t)
                if q // 2 == t // 2:
                    block = 0.5 * (block + raw(t, q).T)
                a_ref[q * n + t] = block

        def step(k, _):
            done = eliminate(a_ref[k * n + k])
            pivots = jnp.sum(jnp.where(row == col, done, 0.0), axis=1, keepdims=True)
            root = jnp.sqrt(pivots)
            upper = jnp.where(col >= row, done, 0.0) / root
            inv = jnp.where(col < row, done, jnp.where(col == row, 1.0, 0.0)) / root
            l_ref[k * n + k] = upper.T
            i_ref[k * n + k] = inv
            for i in range(1, n):

                @pl.when(i > k)
                def _():
                    l_ref[i * n + k] = dot(a_ref[i * n + k], inv, True)

            for i in range(1, n):
                for j in range(1, i + 1):

                    @pl.when(j > k)
                    def _():
                        a_ref[i * n + j] = a_ref[i * n + j] - dot(
                            l_ref[i * n + k], l_ref[j * n + k], True
                        )

            return 0

        lax.fori_loop(0, n, step, 0)
        for i in range(n):
            for j in range(i):
                total = dot(l_ref[i * n + j], i_ref[j * n + j], False)
                for k in range(j + 1, i):
                    total = total + dot(l_ref[i * n + k], i_ref[k * n + j], False)
                i_ref[i * n + j] = -dot(i_ref[i * n + i], total, False)
        zero = jnp.zeros((size, size), jnp.float32)
        for i in range(n):
            for j in range(n):
                rows, cols = slice(i * size, (i + 1) * size), slice(j * size, (j + 1) * size)
                lower_ref[rows, cols] = l_ref[i * n + j] if j <= i else zero
                inverse_ref[rows, cols] = i_ref[i * n + j] if j <= i else zero

    shape = jax.ShapeDtypeStruct((n * size, n * size), jnp.float32)
    blocks = pltpu.VMEM((n * n, size, size), jnp.float32)
    return pl.pallas_call(
        body,
        out_shape=(shape, shape),
        scratch_shapes=[pltpu.VMEM((size * 16, size), jnp.float32), blocks, blocks, blocks],
        compiler_params=pltpu.CompilerParams(vmem_limit_bytes=VMEM_BYTES),
        name="factor_corner",
    )(corner, diagonal)


def update_rows(core, sums, top, other_top, inverse, own_rows, diagonal):
    blocks, n_col, halves, n_rows, lanes = sums.shape
    pairs, top_cols, _, _ = top.shape
    stripes = 2 * pairs
    near = top_cols * lanes
    n_row = stripes // n_col
    share = n_rows // 2 // n_row
    pair = 8 // (blocks * halves)

    def dot(a, b, transposed):
        dims = (((1,), (1 if transposed else 0,)), ((), ()))
        return lax.dot_general(a, b, dims, precision=HIGHEST, preferred_element_type=jnp.float32)

    def body(
        core_ref,
        sums_ref,
        panel_in_ref,
        top_ref,
        other_ref,
        inverse_ref,
        own_ref,
        diag_ref,
        out_ref,
        panel_ref,
        factor_ref,
        flat_ref,
        result_ref,
        mixed_ref,
    ):
        g = pl.program_id(0)
        n_diag = diag_ref.shape[0]
        row = lax.broadcasted_iota(jnp.int32, (n_diag, lanes), 0)

        def with_diagonal(x, t):
            head = x[:n_diag] + jnp.where(row == t, diag_ref[...], 0.0)
            return jnp.concatenate([head, x[n_diag:]], axis=0)

        @pl.when(g == 0)
        def _():
            x = jnp.concatenate(
                [with_diagonal(panel_in_ref[0, t // 2, t % 2], t) for t in range(top_cols)], axis=1
            )
            panel = dot(x, inverse_ref[...], True)
            at = lax.broadcasted_iota(jnp.int32, (8, near), 0)
            head = jnp.where(at < 4, own_ref[...], panel[:8])
            panel = jnp.concatenate([head, panel[8:]], axis=0)
            panel_ref[...] = panel
            factor_ref[...] = dot(panel, inverse_ref[...], False)

        mine, theirs = top_ref[...], other_ref[...]
        first = core_ref[0] == 0
        both = [jnp.where(first, mine, theirs), jnp.where(first, theirs, mine)]
        both = [x.reshape(pairs, 1, top_cols * 8, lanes) for x in both]
        flat_ref[...] = jnp.concatenate(both, axis=1).reshape(stripes * top_cols * 8, lanes)
        for i in range(pair):
            c = g * pair + i
            for cb in range(blocks):
                weights = jnp.concatenate(
                    [
                        jnp.concatenate(
                            [
                                flat_ref[
                                    pl.ds(
                                        k * 8 + (i * blocks + cb) * halves + h,
                                        stripes,
                                        stride=top_cols * 8,
                                    ),
                                    :,
                                ]
                                for k in range(top_cols)
                            ],
                            axis=1,
                        )
                        for h in range(halves)
                    ],
                    axis=0,
                )
                product = dot(factor_ref[...], weights, True)
                for h in range(halves):
                    t = (cb * n_col + c) * halves + h
                    result = with_diagonal(sums_ref[cb, i, h], t)
                    result = result - product[:, h * lanes : (h + 1) * lanes]
                    if cb == 0:
                        at = (i * halves + h) * lanes
                        result = jnp.where(g == 0, panel_ref[:, at : at + lanes], result)
                    result_ref[...] = result
                    for s in range(2):
                        mixed_ref[pl.ds(s * 4 + h * 2 + cb, n_rows // 2, stride=8), :] = result_ref[
                            pl.ds(s, n_rows // 2, stride=2), :
                        ]
            out_ref[:, i] = mixed_ref[...].reshape(n_row, share * 8, lanes)

    def fixed(*shape):
        return pl.BlockSpec(shape, lambda g, core_ref: (0,) * len(shape))

    top_spec = pl.BlockSpec((pairs, top_cols, 8, lanes), lambda g, core_ref: (0, 0, g, 0))
    return pl.pallas_call(
        body,
        grid_spec=pltpu.PrefetchScalarGridSpec(
            num_scalar_prefetch=1,
            grid=(n_col // pair,),
            in_specs=[
                pl.BlockSpec(
                    (blocks, pair, halves, n_rows, lanes), lambda g, core_ref: (0, g, 0, 0, 0)
                ),
                pl.BlockSpec((1, 2, halves, n_rows, lanes), lambda g, core_ref: (0, 0, 0, 0, 0)),
                top_spec,
                top_spec,
                fixed(near, near),
                fixed(8, near),
                fixed(*diagonal.shape),
            ],
            out_specs=pl.BlockSpec(
                (n_row, pair, share * 8, lanes), lambda g, core_ref: (0, g, 0, 0)
            ),
            scratch_shapes=[
                pltpu.VMEM((n_rows, near), jnp.float32),
                pltpu.VMEM((n_rows, near), jnp.float32),
                pltpu.VMEM((stripes * top_cols * 8, lanes), jnp.float32),
                pltpu.VMEM((n_rows, lanes), jnp.float32),
                pltpu.VMEM((n_rows * 4, lanes), jnp.float32),
            ],
        ),
        out_shape=jax.ShapeDtypeStruct((n_row, n_col, share * 8, lanes), jnp.float32),
        compiler_params=pltpu.CompilerParams(vmem_limit_bytes=VMEM_BYTES),
        name="update_rows",
    )(core, sums, sums, top, other_top, inverse, own_rows, diagonal)


def place_rows(received):
    stripes, width, lanes = received.shape
    units = width // 4

    def body(in_ref, out_ref):
        for s in range(2):
            out_ref[s] = in_ref[:, s]

    return pl.pallas_call(
        body,
        grid=(units // 2,),
        in_specs=[pl.BlockSpec((stripes, 2, 4, lanes), lambda g: (0, g, 0, 0))],
        out_specs=pl.BlockSpec((2, stripes, 4, lanes), lambda g: (g, 0, 0, 0)),
        out_shape=jax.ShapeDtypeStruct((units, stripes, 4, lanes), jnp.float32),
        compiler_params=pltpu.CompilerParams(vmem_limit_bytes=VMEM_BYTES),
        name="place_rows",
    )(received.reshape(stripes, units, 4, lanes))


def tile_order(tile_dest, col_tiles, top_rows, top_cols):
    total = tile_dest.shape[0]
    ids = jnp.arange(total, dtype=jnp.int32)
    same = tile_dest[:, None] == tile_dest[None, :]
    first_of = jnp.min(jnp.where(same, ids[None, :], total), axis=1)
    later = jnp.any(jnp.logical_and(same, ids[None, :] > ids[:, None]), axis=1)
    top = jnp.logical_and(tile_dest // col_tiles < top_rows, tile_dest % col_tiles < top_cols)
    rest = jnp.where(
        first_of < ids, 3 * total + first_of, jnp.where(later, total + ids, 2 * total + ids)
    )
    key = jnp.where(top, ids, rest)
    position = jnp.sum((key[None, :] < key[:, None]).astype(jnp.int32), axis=1)
    return (position[:, None] == ids[None, :]).astype(jnp.int32)


def on_device(child_tiles, tile_dest, tile_mask, tile_count, front_diagonal):
    axes = ("row", "col")
    n_row = lax.axis_size("row")
    n_col = lax.axis_size("col")
    devices = n_row * n_col
    me = lax.axis_index("row") * n_col + lax.axis_index("col")
    tile_total, tile_rows, lanes = child_tiles.shape
    col_blocks, panel = front_diagonal.shape
    halves = panel // lanes
    row_tiles = NF // tile_rows
    col_tiles = col_blocks * n_col * halves
    width = col_tiles * lanes
    top_rows = width // tile_rows
    top_cols = 2 * halves

    placed = tile_order(tile_dest, col_tiles, top_rows, top_cols)
    ids = jnp.arange(tile_total, dtype=jnp.int32)
    target = (tile_dest % col_tiles) * row_tiles + tile_dest // col_tiles
    order = jnp.sum(placed * ids[:, None], axis=0)
    target_sent = jnp.sum(placed * target[:, None], axis=0)
    live = (ids < tile_count[0]).astype(jnp.float32)
    mask_columns = lax.dot_general(
        tile_mask.astype(jnp.float32),
        placed.astype(jnp.float32) * live[:, None],
        (((0,), (0,)), ((), ())),
    )
    mask_columns = mask_columns.reshape(tile_rows, tile_total // GROUP, GROUP).transpose(1, 0, 2)
    meta = jnp.concatenate(
        [
            jnp.pad(target_sent.astype(jnp.float32), (0, lanes - tile_total))[None],
            front_diagonal.reshape(col_blocks * halves, lanes),
            jnp.zeros((8 - 1 - col_blocks * halves, lanes), jnp.float32),
        ],
        axis=0,
    )

    def exchange(x):
        return lax.all_to_all(x, axes, split_axis=0, concat_axis=0, tiled=True)

    early = exchange(pack_tiles(order, child_tiles, mask_columns, 0, EARLY, meta))
    at = EARLY
    first_pack = pack_tiles(order, child_tiles, mask_columns, at, CHUNKS[0])
    early, first_pack = lax.optimization_barrier((early, first_pack))

    targets = early[:, 2 * EARLY, :].astype(jnp.int32)
    diagonal = early[:n_col, 2 * EARLY + 1 : 2 * EARLY + 1 + col_blocks * halves, :]
    diagonal = diagonal.reshape(n_col, col_blocks, panel).transpose(1, 0, 2)
    diagonal = diagonal.reshape(col_tiles, lanes)
    early = early.reshape(devices, EARLY + 4, 2, lanes)
    n_top = top_cols * top_rows
    tile, row = targets[:, :EARLY] // row_tiles, targets[:, :EARLY] % row_tiles
    spots = tile * top_rows + row % n_col * col_blocks + row // n_col
    spots = jnp.where(jnp.logical_and(tile < top_cols, row < top_rows), spots, n_top)
    view = add_top(spots, early, n_top)
    view = view.reshape(top_cols, 2 * top_rows, lanes)
    chips = n_col // 2
    my_chip, my_core = lax.axis_index("col") // 2, lax.axis_index("col") % 2
    top = jnp.zeros((chips,) + view.shape, jnp.float32)
    for step in range(chips):
        moved = view
        if step:
            hops = [(2 * i + k, 2 * ((i + step) % chips) + k) for i in range(chips) for k in range(2)]
            moved = lax.ppermute(view, "col", hops)
        origin = (my_chip + chips - step) % chips
        top = lax.dynamic_update_slice(top, moved[None], (origin, 0, 0, 0))
    top, first_pack = lax.optimization_barrier((top, first_pack))
    received0 = exchange(first_pack)
    top = lax.all_gather(top, "row").reshape(devices // 2, top_cols, 2 * top_rows, lanes)

    second_pack = pack_tiles(order, child_tiles, mask_columns, at + CHUNKS[0], CHUNKS[1])
    received0, second_pack = lax.optimization_barrier((received0, second_pack))
    received1 = exchange(second_pack)
    pieces = received0.reshape(devices, CHUNKS[0], 2, lanes)
    sums = add_pieces(targets, pieces, early, None, at, BULK)
    top, sums = lax.optimization_barrier((top, sums))
    swap = [(i, i + 1 - 2 * (i % 2)) for i in range(n_col)]
    other_top = lax.ppermute(top, "col", swap)

    def near_corner(x):
        x = x.reshape(devices // 2, top_cols, n_col, col_blocks, 2, lanes)[:, :, :2, 0]
        return x.reshape(devices // 2, 1, 4 * top_cols, lanes)

    corner = jnp.where(
        my_core == jnp.arange(2).reshape(1, 2, 1, 1), near_corner(top), near_corner(other_top)
    )
    lower, inverse = factor_corner(corner.reshape(devices, 4 * top_cols, lanes), diagonal[:8])
    own_rows = lax.dynamic_slice(
        lower.reshape(top_cols, devices, top_cols * lanes),
        (0, me, 0),
        (top_cols, 1, top_cols * lanes),
    )
    own_rows = jnp.pad(own_rows.reshape(top_cols, top_cols * lanes), ((0, 8 - top_cols), (0, 0)))
    received1, inverse, own_rows = lax.optimization_barrier((received1, inverse, own_rows))
    pieces = received1.reshape(devices, CHUNKS[1], 2, lanes)
    sums = add_pieces(targets, pieces, None, sums, at + CHUNKS[0], BULK)

    own = jnp.where(jnp.arange(lanes, dtype=jnp.int32)[None, :] == me, diagonal, 0.0)
    result = update_rows(
        my_core.reshape(1),
        sums.reshape(col_blocks, n_col, halves, 2 * row_tiles, lanes), top, other_top, inverse, own_rows, own
    )
    received = exchange(result.reshape(devices, -1, lanes))
    rows = place_rows(received)
    rows = rows.reshape(NF // n_row, halves, col_blocks, lanes).transpose(0, 2, 1, 3)
    return rows.reshape(NF // n_row, col_blocks, panel)


def solution(mesh):
    in_specs = (
        P(("row", "col"), None, None),
        P(("row", "col")),
        P(("row", "col"), None),
        P(("row", "col")),
        P(None, "col"),
    )
    out_specs = P("row", None, "col")
    return jax.shard_map(
        on_device, mesh=mesh, in_specs=in_specs, out_specs=out_specs, check_vma=False
    )
```

```python
import jax
import jax.numpy as jnp
from jax import lax
from jax.experimental import pallas as pl
from jax.experimental.pallas import tpu as pltpu
from jax.sharding import PartitionSpec as P

NF = 49152
EARLY = 8
GROUP = 8
CHUNKS = (72, 32)
BULK = 2**31
HIGHEST = lax.Precision.HIGHEST
VMEM_BYTES = 56 * 1024 * 1024


def pack_tiles(order, child_tiles, mask_columns, first, count, meta=None):
    tile_rows, tile_cols = child_tiles.shape[1:]
    stripes = tile_rows // 2
    base = first // GROUP
    extra = 0 if meta is None else meta.shape[0]
    width = 2 * GROUP + extra

    def body(order_ref, *refs):
        tiles, mask_ref = refs[:GROUP], refs[GROUP]
        out_ref, rows_ref = refs[-2], refs[-1]
        for i in range(GROUP):
            for s in range(2):
                rows = tiles[i][0, s * stripes : (s + 1) * stripes, :]
                column = mask_ref[0, s * stripes : (s + 1) * stripes, i : i + 1]
                rows_ref[pl.ds(2 * i + s, stripes, stride=2 * GROUP), :] = rows * column
        out_ref[:, : 2 * GROUP, :] = rows_ref[...].reshape(stripes, 2 * GROUP, tile_cols)
        if extra:
            meta_ref = refs[GROUP + 1]
            out_ref[:, 2 * GROUP :, :] = jnp.broadcast_to(
                meta_ref[...][None], (stripes, extra, tile_cols)
            )

    def tile_spec(i):
        return pl.BlockSpec(
            (1, tile_rows, tile_cols), lambda g, order_ref: (order_ref[first + g * GROUP + i], 0, 0)
        )

    in_specs = [tile_spec(i) for i in range(GROUP)]
    in_specs.append(pl.BlockSpec((1, tile_rows, GROUP), lambda g, order_ref: (base + g, 0, 0)))
    operands = [child_tiles] * GROUP + [mask_columns]
    if extra:
        in_specs.append(pl.BlockSpec((extra, tile_cols), lambda g, order_ref: (0, 0)))
        operands.append(meta)
    steps = count // GROUP
    return pl.pallas_call(
        body,
        grid_spec=pltpu.PrefetchScalarGridSpec(
            num_scalar_prefetch=1,
            grid=(steps,),
            in_specs=in_specs,
            out_specs=pl.BlockSpec((stripes, width, tile_cols), lambda g, order_ref: (0, g, 0)),
            scratch_shapes=[pltpu.VMEM((stripes * 2 * GROUP, tile_cols), jnp.float32)],
        ),
        out_shape=jax.ShapeDtypeStruct((stripes, steps * width, tile_cols), jnp.float32),
        compiler_params=pltpu.CompilerParams(vmem_limit_bytes=VMEM_BYTES),
        name="pack_tiles",
    )(order, *operands)


def add_pieces(targets, pieces, early, sums, first, window, weight):
    sources, count, two, lanes = pieces.shape
    n_sums = 6144
    per_step = 8
    fresh = sums is None

    def body(target_ref, pieces_ref, *refs):
        sums_ref = refs[-1]
        step = pl.program_id(0)

        @pl.when(step == 0)
        def _():
            sums_ref[...] = jnp.zeros_like(sums_ref) if fresh else refs[0][...]

        for n in range(per_step):
            source = step * per_step + n
            if fresh:
                for i in range(EARLY):
                    d = target_ref[source, i]
                    sums_ref[d] = sums_ref[d] + refs[0][n, i]
            for at in range(0, count, window):
                ds = [target_ref[source, first + at + i] for i in range(window)]
                news = [sums_ref[ds[i]] + pieces_ref[n, at + i] for i in range(window)]
                for i in range(window):
                    sums_ref[ds[i]] = news[i]

    def streamed(x):
        return pl.BlockSpec((per_step,) + x.shape[1:], lambda g, target_ref: (g, 0, 0, 0))

    whole = pl.BlockSpec(
        (n_sums, two, lanes), lambda g, target_ref: (0, 0, 0), pipeline_mode=pl.Buffered(1)
    )
    return pl.pallas_call(
        body,
        grid_spec=pltpu.PrefetchScalarGridSpec(
            num_scalar_prefetch=1,
            grid=(sources // per_step,),
            in_specs=[streamed(pieces), streamed(early) if fresh else whole],
            out_specs=whole,
        ),
        out_shape=jax.ShapeDtypeStruct((n_sums, two, lanes), jnp.float32),
        compiler_params=pltpu.CompilerParams(vmem_limit_bytes=VMEM_BYTES),
        cost_estimate=pl.CostEstimate(flops=weight, transcendentals=0, bytes_accessed=weight),
        name="add_pieces",
    )(targets, pieces, early if fresh else sums)


def add_top(spots, pieces, n_sums):
    sources, pitch, two, lanes = pieces.shape
    slots = spots.shape[1]

    def body(spot_ref, pieces_ref, out_ref, *parts):
        for part in parts:
            part[...] = jnp.zeros_like(part)

        def one(source, _):
            for i in range(slots):
                d = spot_ref[source, i]
                parts[i][d] = parts[i][d] + pieces_ref[source, i]
            return 0

        lax.fori_loop(0, sources, one, 0, unroll=4)
        total = parts[0][:n_sums]
        for part in parts[1:]:
            total = total + part[:n_sums]
        out_ref[...] = total

    return pl.pallas_call(
        body,
        grid_spec=pltpu.PrefetchScalarGridSpec(
            num_scalar_prefetch=1,
            grid=(1,),
            in_specs=[pl.BlockSpec(pieces.shape, lambda g, spot_ref: (0, 0, 0, 0))],
            out_specs=pl.BlockSpec((n_sums, two, lanes), lambda g, spot_ref: (0, 0, 0)),
            scratch_shapes=[pltpu.VMEM((n_sums + 8, two, lanes), jnp.float32)] * slots,
        ),
        out_shape=jax.ShapeDtypeStruct((n_sums, two, lanes), jnp.float32),
        compiler_params=pltpu.CompilerParams(vmem_limit_bytes=VMEM_BYTES),
        name="add_top",
    )(spots, pieces)


def factor_corner(corner, diagonal):
    size = corner.shape[2]
    n = 4

    def dot(a, b, transposed):
        dims = (((1,), (1 if transposed else 0,)), ((), ()))
        return lax.dot_general(a, b, dims, precision=HIGHEST, preferred_element_type=jnp.float32)

    def eliminate(block):
        groups = [block[8 * g : 8 * g + 8, :] for g in range(size // 8)]
        lane = lax.broadcasted_iota(jnp.int32, (8, size), 1)
        sub = lax.broadcasted_iota(jnp.int32, (8, size), 0)
        for p in range(size // 8):
            j0 = 8 * p
            rows = [jnp.broadcast_to(groups[p][r : r + 1, :], (8, size)) for r in range(8)]
            entry = [
                [
                    jnp.broadcast_to(rows[r][:, j0 + c : j0 + c + 1], (8, size)) if c >= r else None
                    for c in range(8)
                ]
                for r in range(8)
            ]
            ratio = [[None] * 8 for _ in range(8)]
            scaled = []
            done = groups[p]
            for r in range(8):
                row = jnp.where(jnp.logical_and(lane >= j0, lane < j0 + r), 0.0, rows[r])
                for q in range(r):
                    settled = jnp.logical_and(lane > j0 + q, lane < j0 + r)
                    row = row - ratio[r][q] * jnp.where(settled, 0.0, rows[q])
                done = jnp.where(sub == r, row, done)
                rows[r] = jnp.where(lane == j0 + r, 1.0, row)
                inverse = 1.0 / entry[r][r]
                settled = jnp.logical_and(lane > j0 + r, lane < j0 + 8)
                scaled.append(jnp.where(settled, 0.0, rows[r]) * inverse)
                for c in range(r + 1, 8):
                    ratio[c][r] = entry[r][c] * inverse
                for c in range(r + 1, 8):
                    for d in range(c, 8):
                        entry[c][d] = entry[c][d] - ratio[c][r] * entry[r][d]
            groups[p] = done
            inside = jnp.logical_and(lane >= j0, lane < j0 + 8)
            for g in range(p + 1, size // 8):
                columns = []
                result = jnp.where(inside, 0.0, groups[g])
                for c in range(8):
                    column = jnp.broadcast_to(groups[g][:, j0 + c : j0 + c + 1], (8, size))
                    for q in range(c):
                        column = column - ratio[c][q] * columns[q]
                    columns.append(column)
                    result = result - column * scaled[c]
                groups[g] = result
        return jnp.concatenate(groups, axis=0)

    def body(corner_ref, diag_ref, lower_ref, inverse_ref, flat_ref, a_ref, l_ref, i_ref):
        row = lax.broadcasted_iota(jnp.int32, (size, size), 0)
        col = lax.broadcasted_iota(jnp.int32, (size, size), 1)
        flat_ref[...] = corner_ref[...].reshape(size * 16, size)

        def raw(q, t):
            block = flat_ref[pl.ds(t * 4 + q, size, stride=16), :]
            if q == t:
                block = block + jnp.where(row == col, diag_ref[t : t + 1, :], 0.0)
            return block

        for q in range(n):
            for t in range(q + 1):
                block = raw(q, t)
                if q // 2 == t // 2:
                    block = 0.5 * (block + raw(t, q).T)
                a_ref[q * n + t] = block

        def step(k, _):
            done = eliminate(a_ref[k * n + k])
            pivots = jnp.sum(jnp.where(row == col, done, 0.0), axis=1, keepdims=True)
            root = jnp.sqrt(pivots)
            upper = jnp.where(col >= row, done, 0.0) / root
            inv = jnp.where(col < row, done, jnp.where(col == row, 1.0, 0.0)) / root
            l_ref[k * n + k] = upper.T
            i_ref[k * n + k] = inv
            for i in range(1, n):

                @pl.when(i > k)
                def _():
                    l_ref[i * n + k] = dot(a_ref[i * n + k], inv, True)

            for i in range(1, n):
                for j in range(1, i + 1):

                    @pl.when(j > k)
                    def _():
                        a_ref[i * n + j] = a_ref[i * n + j] - dot(
                            l_ref[i * n + k], l_ref[j * n + k], True
                        )

            return 0

        lax.fori_loop(0, n, step, 0)
        for i in range(n):
            for j in range(i):
                total = dot(l_ref[i * n + j], i_ref[j * n + j], False)
                for k in range(j + 1, i):
                    total = total + dot(l_ref[i * n + k], i_ref[k * n + j], False)
                i_ref[i * n + j] = -dot(i_ref[i * n + i], total, False)
        zero = jnp.zeros((size, size), jnp.float32)
        for i in range(n):
            for j in range(n):
                rows, cols = slice(i * size, (i + 1) * size), slice(j * size, (j + 1) * size)
                lower_ref[rows, cols] = l_ref[i * n + j] if j <= i else zero
                inverse_ref[rows, cols] = i_ref[i * n + j] if j <= i else zero

    shape = jax.ShapeDtypeStruct((n * size, n * size), jnp.float32)
    blocks = pltpu.VMEM((n * n, size, size), jnp.float32)
    return pl.pallas_call(
        body,
        out_shape=(shape, shape),
        scratch_shapes=[pltpu.VMEM((size * 16, size), jnp.float32), blocks, blocks, blocks],
        compiler_params=pltpu.CompilerParams(vmem_limit_bytes=VMEM_BYTES),
        name="factor_corner",
    )(corner, diagonal)


def update_rows(core, sums, top, other_top, inverse, own_rows, diagonal):
    blocks, n_col, halves, n_rows, lanes = sums.shape
    pairs, top_cols, _, _ = top.shape
    stripes = 2 * pairs
    near = top_cols * lanes
    n_row = stripes // n_col
    share = n_rows // 2 // n_row
    pair = 8 // (blocks * halves)

    def dot(a, b, transposed):
        dims = (((1,), (1 if transposed else 0,)), ((), ()))
        precision = HIGHEST if a.dtype == jnp.float32 else None
        return lax.dot_general(a, b, dims, precision=precision, preferred_element_type=jnp.float32)

    def body(
        core_ref,
        sums_ref,
        panel_in_ref,
        top_ref,
        other_ref,
        inverse_ref,
        own_ref,
        diag_ref,
        out_ref,
        panel_ref,
        high_ref,
        low_ref,
        flat_ref,
        result_ref,
        mixed_ref,
    ):
        g = pl.program_id(0)
        n_diag = diag_ref.shape[0]
        row = lax.broadcasted_iota(jnp.int32, (n_diag, lanes), 0)

        def with_diagonal(x, t):
            head = x[:n_diag] + jnp.where(row == t, diag_ref[...], 0.0)
            return jnp.concatenate([head, x[n_diag:]], axis=0)

        @pl.when(g == 0)
        def _():
            x = jnp.concatenate(
                [with_diagonal(panel_in_ref[0, t // 2, t % 2], t) for t in range(top_cols)], axis=1
            )
            panel = dot(x, inverse_ref[...], True)
            at = lax.broadcasted_iota(jnp.int32, (8, near), 0)
            head = jnp.where(at < 4, own_ref[...], panel[:8])
            panel = jnp.concatenate([head, panel[8:]], axis=0)
            panel_ref[...] = panel
            factor = dot(panel, inverse_ref[...], False)
            high_ref[...] = factor.astype(jnp.bfloat16)
            low_ref[...] = (factor - high_ref[...].astype(jnp.float32)).astype(jnp.bfloat16)

        mine, theirs = top_ref[...], other_ref[...]
        first = core_ref[0] == 0
        both = [jnp.where(first, mine, theirs), jnp.where(first, theirs, mine)]
        both = [x.reshape(pairs, 1, top_cols * 8, lanes) for x in both]
        flat_ref[...] = jnp.concatenate(both, axis=1).reshape(stripes * top_cols * 8, lanes)
        for i in range(pair):
            c = g * pair + i
            for cb in range(blocks):
                weights = jnp.concatenate(
                    [
                        jnp.concatenate(
                            [
                                flat_ref[
                                    pl.ds(
                                        k * 8 + (i * blocks + cb) * halves + h,
                                        stripes,
                                        stride=top_cols * 8,
                                    ),
                                    :,
                                ]
                                for k in range(top_cols)
                            ],
                            axis=1,
                        )
                        for h in range(halves)
                    ],
                    axis=0,
                )
                high = weights.astype(jnp.bfloat16)
                low = (weights - high.astype(jnp.float32)).astype(jnp.bfloat16)
                product = dot(low_ref[...], high, True) + dot(high_ref[...], low, True)
                product = product + dot(high_ref[...], high, True)
                for h in range(halves):
                    t = (cb * n_col + c) * halves + h
                    result = with_diagonal(sums_ref[cb, i, h], t)
                    result = result - product[:, h * lanes : (h + 1) * lanes]
                    if cb == 0:
                        at = (i * halves + h) * lanes
                        result = jnp.where(g == 0, panel_ref[:, at : at + lanes], result)
                    result_ref[...] = result
                    for s in range(2):
                        mixed_ref[pl.ds(s * 4 + h * 2 + cb, n_rows // 2, stride=8), :] = result_ref[
                            pl.ds(s, n_rows // 2, stride=2), :
                        ]
            out_ref[:, i] = mixed_ref[...].reshape(n_row, share * 8, lanes)

    def fixed(*shape):
        return pl.BlockSpec(shape, lambda g, core_ref: (0,) * len(shape))

    top_spec = pl.BlockSpec((pairs, top_cols, 8, lanes), lambda g, core_ref: (0, 0, g, 0))
    return pl.pallas_call(
        body,
        grid_spec=pltpu.PrefetchScalarGridSpec(
            num_scalar_prefetch=1,
            grid=(n_col // pair,),
            in_specs=[
                pl.BlockSpec(
                    (blocks, pair, halves, n_rows, lanes), lambda g, core_ref: (0, g, 0, 0, 0)
                ),
                pl.BlockSpec((1, 2, halves, n_rows, lanes), lambda g, core_ref: (0, 0, 0, 0, 0)),
                top_spec,
                top_spec,
                fixed(near, near),
                fixed(8, near),
                fixed(*diagonal.shape),
            ],
            out_specs=pl.BlockSpec(
                (n_row, pair, share * 8, lanes), lambda g, core_ref: (0, g, 0, 0)
            ),
            scratch_shapes=[
                pltpu.VMEM((n_rows, near), jnp.float32),
                pltpu.VMEM((n_rows, near), jnp.bfloat16),
                pltpu.VMEM((n_rows, near), jnp.bfloat16),
                pltpu.VMEM((stripes * top_cols * 8, lanes), jnp.float32),
                pltpu.VMEM((n_rows, lanes), jnp.float32),
                pltpu.VMEM((n_rows * 4, lanes), jnp.float32),
            ],
        ),
        out_shape=jax.ShapeDtypeStruct((n_row, n_col, share * 8, lanes), jnp.float32),
        compiler_params=pltpu.CompilerParams(vmem_limit_bytes=VMEM_BYTES),
        name="update_rows",
    )(core, sums, sums, top, other_top, inverse, own_rows, diagonal)


def place_rows(received):
    stripes, width, lanes = received.shape
    units = width // 4
    share = units // 2

    def body(in_ref, out_ref):
        for s in range(share):
            out_ref[s] = in_ref[:, s]

    return pl.pallas_call(
        body,
        grid=(units // share,),
        in_specs=[pl.BlockSpec((stripes, share, 4, lanes), lambda g: (0, g, 0, 0))],
        out_specs=pl.BlockSpec((share, stripes, 4, lanes), lambda g: (g, 0, 0, 0)),
        out_shape=jax.ShapeDtypeStruct((units, stripes, 4, lanes), jnp.float32),
        compiler_params=pltpu.CompilerParams(vmem_limit_bytes=VMEM_BYTES),
        name="place_rows",
    )(received.reshape(stripes, units, 4, lanes))


def tile_order(tile_dest, col_tiles, top_rows, top_cols):
    total = tile_dest.shape[0]
    ids = jnp.arange(total, dtype=jnp.int32)
    same = tile_dest[:, None] == tile_dest[None, :]
    first_of = jnp.min(jnp.where(same, ids[None, :], total), axis=1)
    later = jnp.any(jnp.logical_and(same, ids[None, :] > ids[:, None]), axis=1)
    top = jnp.logical_and(tile_dest // col_tiles < top_rows, tile_dest % col_tiles < top_cols)
    rest = jnp.where(
        first_of < ids, 3 * total + first_of, jnp.where(later, total + ids, 2 * total + ids)
    )
    key = jnp.where(top, ids, rest)
    position = jnp.sum((key[None, :] < key[:, None]).astype(jnp.int32), axis=1)
    return (position[:, None] == ids[None, :]).astype(jnp.int32)


def on_device(child_tiles, tile_dest, tile_mask, tile_count, front_diagonal):
    axes = ("row", "col")
    n_row = lax.axis_size("row")
    n_col = lax.axis_size("col")
    devices = n_row * n_col
    me = lax.axis_index("row") * n_col + lax.axis_index("col")
    tile_total, tile_rows, lanes = child_tiles.shape
    col_blocks, panel = front_diagonal.shape
    halves = panel // lanes
    row_tiles = NF // tile_rows
    col_tiles = col_blocks * n_col * halves
    width = col_tiles * lanes
    top_rows = width // tile_rows
    top_cols = 2 * halves

    placed = tile_order(tile_dest, col_tiles, top_rows, top_cols)
    ids = jnp.arange(tile_total, dtype=jnp.int32)
    target = (tile_dest % col_tiles) * row_tiles + tile_dest // col_tiles
    order = jnp.sum(placed * ids[:, None], axis=0)
    target_sent = jnp.sum(placed * target[:, None], axis=0)
    live = (ids < tile_count[0]).astype(jnp.float32)
    mask_columns = lax.dot_general(
        tile_mask.astype(jnp.float32),
        placed.astype(jnp.float32) * live[:, None],
        (((0,), (0,)), ((), ())),
    )
    mask_columns = mask_columns.reshape(tile_rows, tile_total // GROUP, GROUP).transpose(1, 0, 2)
    meta = jnp.concatenate(
        [
            jnp.pad(target_sent.astype(jnp.float32), (0, lanes - tile_total))[None],
            front_diagonal.reshape(col_blocks * halves, lanes),
            jnp.zeros((8 - 1 - col_blocks * halves, lanes), jnp.float32),
        ],
        axis=0,
    )

    def exchange(x):
        return lax.all_to_all(x, axes, split_axis=0, concat_axis=0, tiled=True)

    early = exchange(pack_tiles(order, child_tiles, mask_columns, 0, EARLY, meta))
    at = EARLY
    first_pack = pack_tiles(order, child_tiles, mask_columns, at, CHUNKS[0])
    early, first_pack = lax.optimization_barrier((early, first_pack))

    targets = early[:, 2 * EARLY, :].astype(jnp.int32)
    diagonal = early[:n_col, 2 * EARLY + 1 : 2 * EARLY + 1 + col_blocks * halves, :]
    diagonal = diagonal.reshape(n_col, col_blocks, panel).transpose(1, 0, 2)
    diagonal = diagonal.reshape(col_tiles, lanes)
    early = early.reshape(devices, EARLY + 4, 2, lanes)
    n_top = top_cols * top_rows
    tile, row = targets[:, :EARLY] // row_tiles, targets[:, :EARLY] % row_tiles
    spots = tile * top_rows + row % n_col * col_blocks + row // n_col
    spots = jnp.where(jnp.logical_and(tile < top_cols, row < top_rows), spots, n_top)
    view = add_top(spots, early, n_top)
    view = view.reshape(top_cols, 2 * top_rows, lanes)
    chips = n_col // 2
    my_chip, my_core = lax.axis_index("col") // 2, lax.axis_index("col") % 2
    top = jnp.zeros((chips,) + view.shape, jnp.float32)
    for step in range(chips):
        moved = view
        if step:
            hops = [(2 * i + k, 2 * ((i + step) % chips) + k) for i in range(chips) for k in range(2)]
            moved = lax.ppermute(view, "col", hops)
        origin = (my_chip + chips - step) % chips
        top = lax.dynamic_update_slice(top, moved[None], (origin, 0, 0, 0))
    top, first_pack = lax.optimization_barrier((top, first_pack))
    received0 = exchange(first_pack)
    top = lax.all_gather(top, "row").reshape(devices // 2, top_cols, 2 * top_rows, lanes)

    second_pack = pack_tiles(order, child_tiles, mask_columns, at + CHUNKS[0], CHUNKS[1])
    received0, second_pack = lax.optimization_barrier((received0, second_pack))
    received1 = exchange(second_pack)
    pieces = received0.reshape(devices, CHUNKS[0], 2, lanes)
    sums = add_pieces(targets, pieces, early, None, at, 12, BULK)
    top, sums = lax.optimization_barrier((top, sums))
    swap = [(i, i + 1 - 2 * (i % 2)) for i in range(n_col)]
    other_top = lax.ppermute(top, "col", swap)

    def near_corner(x):
        x = x.reshape(devices // 2, top_cols, n_col, col_blocks, 2, lanes)[:, :, :2, 0]
        return x.reshape(devices // 2, 1, 4 * top_cols, lanes)

    corner = jnp.where(
        my_core == jnp.arange(2).reshape(1, 2, 1, 1), near_corner(top), near_corner(other_top)
    )
    lower, inverse = factor_corner(corner.reshape(devices, 4 * top_cols, lanes), diagonal[:8])
    own_rows = lax.dynamic_slice(
        lower.reshape(top_cols, devices, top_cols * lanes),
        (0, me, 0),
        (top_cols, 1, top_cols * lanes),
    )
    own_rows = jnp.pad(own_rows.reshape(top_cols, top_cols * lanes), ((0, 8 - top_cols), (0, 0)))
    received1, inverse, own_rows = lax.optimization_barrier((received1, inverse, own_rows))
    pieces = received1.reshape(devices, CHUNKS[1], 2, lanes)
    sums = add_pieces(targets, pieces, None, sums, at + CHUNKS[0], 16, BULK)

    own = jnp.where(jnp.arange(lanes, dtype=jnp.int32)[None, :] == me, diagonal, 0.0)
    result = update_rows(
        my_core.reshape(1),
        sums.reshape(col_blocks, n_col, halves, 2 * row_tiles, lanes), top, other_top, inverse, own_rows, own
    )
    received = exchange(result.reshape(devices, -1, lanes))
    rows = place_rows(received)
    rows = rows.reshape(NF // n_row, halves, col_blocks, lanes).transpose(0, 2, 1, 3)
    return rows.reshape(NF // n_row, col_blocks, panel)


def solution(mesh):
    in_specs = (
        P(("row", "col"), None, None),
        P(("row", "col")),
        P(("row", "col"), None),
        P(("row", "col")),
        P(None, "col"),
    )
    out_specs = P("row", None, "col")
    return jax.shard_map(
        on_device, mesh=mesh, in_specs=in_specs, out_specs=out_specs, check_vma=False
    )
```

```python
import jax
import jax.numpy as jnp
from jax import lax
from jax.experimental import pallas as pl
from jax.experimental.pallas import tpu as pltpu
from jax.sharding import PartitionSpec as P

NF = 49152
EARLY = 8
GROUP = 8
CHUNKS = (64, 40)
BULK = 2**31
HIGHEST = lax.Precision.HIGHEST
VMEM_BYTES = 56 * 1024 * 1024


def pack_tiles(order, child_tiles, mask_columns, first, count, meta=None):
    tile_rows, tile_cols = child_tiles.shape[1:]
    stripes = tile_rows // 2
    base = first // GROUP
    extra = 0 if meta is None else meta.shape[0]
    width = 2 * GROUP + extra

    def body(order_ref, *refs):
        tiles, mask_ref = refs[:GROUP], refs[GROUP]
        out_ref, rows_ref = refs[-2], refs[-1]
        for i in range(GROUP):
            for s in range(2):
                rows = tiles[i][0, s * stripes : (s + 1) * stripes, :]
                column = mask_ref[0, s * stripes : (s + 1) * stripes, i : i + 1]
                rows_ref[pl.ds(2 * i + s, stripes, stride=2 * GROUP), :] = rows * column
        out_ref[:, : 2 * GROUP, :] = rows_ref[...].reshape(stripes, 2 * GROUP, tile_cols)
        if extra:
            meta_ref = refs[GROUP + 1]
            out_ref[:, 2 * GROUP :, :] = jnp.broadcast_to(
                meta_ref[...][None], (stripes, extra, tile_cols)
            )

    def tile_spec(i):
        return pl.BlockSpec(
            (1, tile_rows, tile_cols), lambda g, order_ref: (order_ref[first + g * GROUP + i], 0, 0)
        )

    in_specs = [tile_spec(i) for i in range(GROUP)]
    in_specs.append(pl.BlockSpec((1, tile_rows, GROUP), lambda g, order_ref: (base + g, 0, 0)))
    operands = [child_tiles] * GROUP + [mask_columns]
    if extra:
        in_specs.append(pl.BlockSpec((extra, tile_cols), lambda g, order_ref: (0, 0)))
        operands.append(meta)
    steps = count // GROUP
    return pl.pallas_call(
        body,
        grid_spec=pltpu.PrefetchScalarGridSpec(
            num_scalar_prefetch=1,
            grid=(steps,),
            in_specs=in_specs,
            out_specs=pl.BlockSpec((stripes, width, tile_cols), lambda g, order_ref: (0, g, 0)),
            scratch_shapes=[pltpu.VMEM((stripes * 2 * GROUP, tile_cols), jnp.float32)],
        ),
        out_shape=jax.ShapeDtypeStruct((stripes, steps * width, tile_cols), jnp.float32),
        compiler_params=pltpu.CompilerParams(vmem_limit_bytes=VMEM_BYTES),
        name="pack_tiles",
    )(order, *operands)


def add_pieces(targets, pieces, early, sums, first, window, weight):
    sources, count, two, lanes = pieces.shape
    n_sums = 6144
    per_step = 8
    fresh = sums is None

    def body(target_ref, pieces_ref, *refs):
        sums_ref = refs[-1]
        step = pl.program_id(0)

        @pl.when(step == 0)
        def _():
            sums_ref[...] = jnp.zeros_like(sums_ref) if fresh else refs[0][...]

        for n in range(per_step):
            source = step * per_step + n
            if fresh:
                for i in range(EARLY):
                    d = target_ref[source, i]
                    sums_ref[d] = sums_ref[d] + refs[0][n, i]
            for at in range(0, count, window):
                ds = [target_ref[source, first + at + i] for i in range(window)]
                news = [sums_ref[ds[i]] + pieces_ref[n, at + i] for i in range(window)]
                for i in range(window):
                    sums_ref[ds[i]] = news[i]

    def streamed(x):
        return pl.BlockSpec((per_step,) + x.shape[1:], lambda g, target_ref: (g, 0, 0, 0))

    whole = pl.BlockSpec(
        (n_sums, two, lanes), lambda g, target_ref: (0, 0, 0), pipeline_mode=pl.Buffered(1)
    )
    return pl.pallas_call(
        body,
        grid_spec=pltpu.PrefetchScalarGridSpec(
            num_scalar_prefetch=1,
            grid=(sources // per_step,),
            in_specs=[streamed(pieces), streamed(early) if fresh else whole],
            out_specs=whole,
        ),
        out_shape=jax.ShapeDtypeStruct((n_sums, two, lanes), jnp.float32),
        compiler_params=pltpu.CompilerParams(vmem_limit_bytes=VMEM_BYTES),
        cost_estimate=pl.CostEstimate(flops=weight, transcendentals=0, bytes_accessed=weight),
        name="add_pieces",
    )(targets, pieces, early if fresh else sums)


def add_top(spots, pieces, n_sums):
    sources, pitch, two, lanes = pieces.shape
    slots = spots.shape[1]

    def body(spot_ref, pieces_ref, out_ref, *parts):
        for part in parts:
            part[...] = jnp.zeros_like(part)

        def one(source, _):
            for i in range(slots):
                d = spot_ref[source, i]
                parts[i][d] = parts[i][d] + pieces_ref[source, i]
            return 0

        lax.fori_loop(0, sources, one, 0, unroll=4)
        total = parts[0][:n_sums]
        for part in parts[1:]:
            total = total + part[:n_sums]
        out_ref[...] = total

    return pl.pallas_call(
        body,
        grid_spec=pltpu.PrefetchScalarGridSpec(
            num_scalar_prefetch=1,
            grid=(1,),
            in_specs=[pl.BlockSpec(pieces.shape, lambda g, spot_ref: (0, 0, 0, 0))],
            out_specs=pl.BlockSpec((n_sums, two, lanes), lambda g, spot_ref: (0, 0, 0)),
            scratch_shapes=[pltpu.VMEM((n_sums + 8, two, lanes), jnp.float32)] * slots,
        ),
        out_shape=jax.ShapeDtypeStruct((n_sums, two, lanes), jnp.float32),
        compiler_params=pltpu.CompilerParams(vmem_limit_bytes=VMEM_BYTES),
        name="add_top",
    )(spots, pieces)


def factor_corner(corner, diagonal):
    size = corner.shape[2]
    n = 4

    def dot(a, b, transposed):
        dims = (((1,), (1 if transposed else 0,)), ((), ()))
        return lax.dot_general(a, b, dims, precision=HIGHEST, preferred_element_type=jnp.float32)

    def eliminate(block):
        groups = [block[8 * g : 8 * g + 8, :] for g in range(size // 8)]
        lane = lax.broadcasted_iota(jnp.int32, (8, size), 1)
        sub = lax.broadcasted_iota(jnp.int32, (8, size), 0)
        for p in range(size // 8):
            j0 = 8 * p
            rows = [jnp.broadcast_to(groups[p][r : r + 1, :], (8, size)) for r in range(8)]
            entry = [
                [
                    jnp.broadcast_to(rows[r][:, j0 + c : j0 + c + 1], (8, size)) if c >= r else None
                    for c in range(8)
                ]
                for r in range(8)
            ]
            ratio = [[None] * 8 for _ in range(8)]
            scaled = []
            done = groups[p]
            for r in range(8):
                row = jnp.where(jnp.logical_and(lane >= j0, lane < j0 + r), 0.0, rows[r])
                for q in range(r):
                    settled = jnp.logical_and(lane > j0 + q, lane < j0 + r)
                    row = row - ratio[r][q] * jnp.where(settled, 0.0, rows[q])
                done = jnp.where(sub == r, row, done)
                rows[r] = jnp.where(lane == j0 + r, 1.0, row)
                inverse = 1.0 / entry[r][r]
                settled = jnp.logical_and(lane > j0 + r, lane < j0 + 8)
                scaled.append(jnp.where(settled, 0.0, rows[r]) * inverse)
                for c in range(r + 1, 8):
                    ratio[c][r] = entry[r][c] * inverse
                for c in range(r + 1, 8):
                    for d in range(c, 8):
                        entry[c][d] = entry[c][d] - ratio[c][r] * entry[r][d]
            groups[p] = done
            inside = jnp.logical_and(lane >= j0, lane < j0 + 8)
            for g in range(p + 1, size // 8):
                columns = []
                result = jnp.where(inside, 0.0, groups[g])
                for c in range(8):
                    column = jnp.broadcast_to(groups[g][:, j0 + c : j0 + c + 1], (8, size))
                    for q in range(c):
                        column = column - ratio[c][q] * columns[q]
                    columns.append(column)
                    result = result - column * scaled[c]
                groups[g] = result
        return jnp.concatenate(groups, axis=0)

    def body(corner_ref, diag_ref, lower_ref, inverse_ref, flat_ref, a_ref, l_ref, i_ref):
        row = lax.broadcasted_iota(jnp.int32, (size, size), 0)
        col = lax.broadcasted_iota(jnp.int32, (size, size), 1)
        flat_ref[...] = corner_ref[...].reshape(size * 16, size)

        def raw(q, t):
            block = flat_ref[pl.ds(t * 4 + q, size, stride=16), :]
            if q == t:
                block = block + jnp.where(row == col, diag_ref[t : t + 1, :], 0.0)
            return block

        for q in range(n):
            for t in range(q + 1):
                block = raw(q, t)
                if q // 2 == t // 2:
                    block = 0.5 * (block + raw(t, q).T)
                a_ref[q * n + t] = block

        def step(k, _):
            done = eliminate(a_ref[k * n + k])
            pivots = jnp.sum(jnp.where(row == col, done, 0.0), axis=1, keepdims=True)
            root = jnp.sqrt(pivots)
            upper = jnp.where(col >= row, done, 0.0) / root
            inv = jnp.where(col < row, done, jnp.where(col == row, 1.0, 0.0)) / root
            l_ref[k * n + k] = upper.T
            i_ref[k * n + k] = inv
            for i in range(1, n):

                @pl.when(i > k)
                def _():
                    l_ref[i * n + k] = dot(a_ref[i * n + k], inv, True)

            for i in range(1, n):
                for j in range(1, i + 1):

                    @pl.when(j > k)
                    def _():
                        a_ref[i * n + j] = a_ref[i * n + j] - dot(
                            l_ref[i * n + k], l_ref[j * n + k], True
                        )

            return 0

        lax.fori_loop(0, n, step, 0)
        for i in range(n):
            for j in range(i):
                total = dot(l_ref[i * n + j], i_ref[j * n + j], False)
                for k in range(j + 1, i):
                    total = total + dot(l_ref[i * n + k], i_ref[k * n + j], False)
                i_ref[i * n + j] = -dot(i_ref[i * n + i], total, False)
        zero = jnp.zeros((size, size), jnp.float32)
        for i in range(n):
            for j in range(n):
                rows, cols = slice(i * size, (i + 1) * size), slice(j * size, (j + 1) * size)
                lower_ref[rows, cols] = l_ref[i * n + j] if j <= i else zero
                inverse_ref[rows, cols] = i_ref[i * n + j] if j <= i else zero

    shape = jax.ShapeDtypeStruct((n * size, n * size), jnp.float32)
    blocks = pltpu.VMEM((n * n, size, size), jnp.float32)
    return pl.pallas_call(
        body,
        out_shape=(shape, shape),
        scratch_shapes=[pltpu.VMEM((size * 16, size), jnp.float32), blocks, blocks, blocks],
        compiler_params=pltpu.CompilerParams(vmem_limit_bytes=VMEM_BYTES),
        name="factor_corner",
    )(corner, diagonal)


def update_rows(core, sums, top, other_top, inverse, own_rows, diagonal):
    blocks, n_col, halves, n_rows, lanes = sums.shape
    pairs, top_cols, _, _ = top.shape
    stripes = 2 * pairs
    near = top_cols * lanes
    n_row = stripes // n_col
    share = n_rows // 2 // n_row
    pair = 8 // (blocks * halves)

    def dot(a, b, transposed):
        dims = (((1,), (1 if transposed else 0,)), ((), ()))
        precision = HIGHEST if a.dtype == jnp.float32 else None
        return lax.dot_general(a, b, dims, precision=precision, preferred_element_type=jnp.float32)

    def body(
        core_ref,
        sums_ref,
        panel_in_ref,
        top_ref,
        other_ref,
        inverse_ref,
        own_ref,
        diag_ref,
        out_ref,
        panel_ref,
        high_ref,
        low_ref,
        flat_ref,
        result_ref,
        mixed_ref,
    ):
        g = pl.program_id(0)
        n_diag = diag_ref.shape[0]
        row = lax.broadcasted_iota(jnp.int32, (n_diag, lanes), 0)

        def with_diagonal(x, t):
            head = x[:n_diag] + jnp.where(row == t, diag_ref[...], 0.0)
            return jnp.concatenate([head, x[n_diag:]], axis=0)

        @pl.when(g == 0)
        def _():
            x = jnp.concatenate(
                [with_diagonal(panel_in_ref[0, t // 2, t % 2], t) for t in range(top_cols)], axis=1
            )
            panel = dot(x, inverse_ref[...], True)
            at = lax.broadcasted_iota(jnp.int32, (8, near), 0)
            head = jnp.where(at < 4, own_ref[...], panel[:8])
            panel = jnp.concatenate([head, panel[8:]], axis=0)
            panel_ref[...] = panel
            factor = dot(panel, inverse_ref[...], False)
            high_ref[...] = factor.astype(jnp.bfloat16)
            low_ref[...] = (factor - high_ref[...].astype(jnp.float32)).astype(jnp.bfloat16)

        mine, theirs = top_ref[...], other_ref[...]
        first = core_ref[0] == 0
        both = [jnp.where(first, mine, theirs), jnp.where(first, theirs, mine)]
        both = [x.reshape(pairs, 1, top_cols * 8, lanes) for x in both]
        flat_ref[...] = jnp.concatenate(both, axis=1).reshape(stripes * top_cols * 8, lanes)
        for i in range(pair):
            c = g * pair + i
            for cb in range(blocks):
                weights = jnp.concatenate(
                    [
                        jnp.concatenate(
                            [
                                flat_ref[
                                    pl.ds(
                                        k * 8 + (i * blocks + cb) * halves + h,
                                        stripes,
                                        stride=top_cols * 8,
                                    ),
                                    :,
                                ]
                                for k in range(top_cols)
                            ],
                            axis=1,
                        )
                        for h in range(halves)
                    ],
                    axis=0,
                )
                high = weights.astype(jnp.bfloat16)
                low = (weights - high.astype(jnp.float32)).astype(jnp.bfloat16)
                product = dot(low_ref[...], high, True) + dot(high_ref[...], low, True)
                product = product + dot(high_ref[...], high, True)
                for h in range(halves):
                    t = (cb * n_col + c) * halves + h
                    result = with_diagonal(sums_ref[cb, i, h], t)
                    result = result - product[:, h * lanes : (h + 1) * lanes]
                    if cb == 0:
                        at = (i * halves + h) * lanes
                        result = jnp.where(g == 0, panel_ref[:, at : at + lanes], result)
                    result_ref[...] = result
                    for s in range(2):
                        mixed_ref[pl.ds(s * 4 + h * 2 + cb, n_rows // 2, stride=8), :] = result_ref[
                            pl.ds(s, n_rows // 2, stride=2), :
                        ]
            out_ref[:, i] = mixed_ref[...].reshape(n_row, share * 8, lanes)

    def fixed(*shape):
        return pl.BlockSpec(shape, lambda g, core_ref: (0,) * len(shape))

    top_spec = pl.BlockSpec((pairs, top_cols, 8, lanes), lambda g, core_ref: (0, 0, g, 0))
    return pl.pallas_call(
        body,
        grid_spec=pltpu.PrefetchScalarGridSpec(
            num_scalar_prefetch=1,
            grid=(n_col // pair,),
            in_specs=[
                pl.BlockSpec(
                    (blocks, pair, halves, n_rows, lanes), lambda g, core_ref: (0, g, 0, 0, 0)
                ),
                pl.BlockSpec((1, 2, halves, n_rows, lanes), lambda g, core_ref: (0, 0, 0, 0, 0)),
                top_spec,
                top_spec,
                fixed(near, near),
                fixed(8, near),
                fixed(*diagonal.shape),
            ],
            out_specs=pl.BlockSpec(
                (n_row, pair, share * 8, lanes), lambda g, core_ref: (0, g, 0, 0)
            ),
            scratch_shapes=[
                pltpu.VMEM((n_rows, near), jnp.float32),
                pltpu.VMEM((n_rows, near), jnp.bfloat16),
                pltpu.VMEM((n_rows, near), jnp.bfloat16),
                pltpu.VMEM((stripes * top_cols * 8, lanes), jnp.float32),
                pltpu.VMEM((n_rows, lanes), jnp.float32),
                pltpu.VMEM((n_rows * 4, lanes), jnp.float32),
            ],
        ),
        out_shape=jax.ShapeDtypeStruct((n_row, n_col, share * 8, lanes), jnp.float32),
        compiler_params=pltpu.CompilerParams(vmem_limit_bytes=VMEM_BYTES),
        name="update_rows",
    )(core, sums, sums, top, other_top, inverse, own_rows, diagonal)


def place_rows(received):
    stripes, width, lanes = received.shape
    units = width // 4
    share = units // 2

    def body(in_ref, out_ref):
        for s in range(share):
            out_ref[s] = in_ref[:, s]

    return pl.pallas_call(
        body,
        grid=(units // share,),
        in_specs=[pl.BlockSpec((stripes, share, 4, lanes), lambda g: (0, g, 0, 0))],
        out_specs=pl.BlockSpec((share, stripes, 4, lanes), lambda g: (g, 0, 0, 0)),
        out_shape=jax.ShapeDtypeStruct((units, stripes, 4, lanes), jnp.float32),
        compiler_params=pltpu.CompilerParams(vmem_limit_bytes=VMEM_BYTES),
        name="place_rows",
    )(received.reshape(stripes, units, 4, lanes))


def tile_order(tile_dest, col_tiles, top_rows, top_cols):
    total = tile_dest.shape[0]
    ids = jnp.arange(total, dtype=jnp.int32)
    same = tile_dest[:, None] == tile_dest[None, :]
    first_of = jnp.min(jnp.where(same, ids[None, :], total), axis=1)
    later = jnp.any(jnp.logical_and(same, ids[None, :] > ids[:, None]), axis=1)
    top = jnp.logical_and(tile_dest // col_tiles < top_rows, tile_dest % col_tiles < top_cols)
    rest = jnp.where(
        first_of < ids, 3 * total + first_of, jnp.where(later, total + ids, 2 * total + ids)
    )
    key = jnp.where(top, ids, rest)
    position = jnp.sum((key[None, :] < key[:, None]).astype(jnp.int32), axis=1)
    return (position[:, None] == ids[None, :]).astype(jnp.int32)


def on_device(child_tiles, tile_dest, tile_mask, tile_count, front_diagonal):
    axes = ("row", "col")
    n_row = lax.axis_size("row")
    n_col = lax.axis_size("col")
    devices = n_row * n_col
    me = lax.axis_index("row") * n_col + lax.axis_index("col")
    tile_total, tile_rows, lanes = child_tiles.shape
    col_blocks, panel = front_diagonal.shape
    halves = panel // lanes
    row_tiles = NF // tile_rows
    col_tiles = col_blocks * n_col * halves
    width = col_tiles * lanes
    top_rows = width // tile_rows
    top_cols = 2 * halves

    placed = tile_order(tile_dest, col_tiles, top_rows, top_cols)
    ids = jnp.arange(tile_total, dtype=jnp.int32)
    target = (tile_dest % col_tiles) * row_tiles + tile_dest // col_tiles
    order = jnp.sum(placed * ids[:, None], axis=0)
    target_sent = jnp.sum(placed * target[:, None], axis=0)
    live = (ids < tile_count[0]).astype(jnp.float32)
    mask_columns = lax.dot_general(
        tile_mask.astype(jnp.float32),
        placed.astype(jnp.float32) * live[:, None],
        (((0,), (0,)), ((), ())),
    )
    mask_columns = mask_columns.reshape(tile_rows, tile_total // GROUP, GROUP).transpose(1, 0, 2)
    meta = jnp.concatenate(
        [
            jnp.pad(target_sent.astype(jnp.float32), (0, lanes - tile_total))[None],
            front_diagonal.reshape(col_blocks * halves, lanes),
            jnp.zeros((8 - 1 - col_blocks * halves, lanes), jnp.float32),
        ],
        axis=0,
    )

    def exchange(x):
        return lax.all_to_all(x, axes, split_axis=0, concat_axis=0, tiled=True)

    early = exchange(pack_tiles(order, child_tiles, mask_columns, 0, EARLY, meta))
    at = EARLY
    first_pack = pack_tiles(order, child_tiles, mask_columns, at, CHUNKS[0])
    early, first_pack = lax.optimization_barrier((early, first_pack))

    targets = early[:, 2 * EARLY, :].astype(jnp.int32)
    diagonal = early[:n_col, 2 * EARLY + 1 : 2 * EARLY + 1 + col_blocks * halves, :]
    diagonal = diagonal.reshape(n_col, col_blocks, panel).transpose(1, 0, 2)
    diagonal = diagonal.reshape(col_tiles, lanes)
    early = early.reshape(devices, EARLY + 4, 2, lanes)
    n_top = top_cols * top_rows
    tile, row = targets[:, :EARLY] // row_tiles, targets[:, :EARLY] % row_tiles
    spots = tile * top_rows + row % n_col * col_blocks + row // n_col
    spots = jnp.where(jnp.logical_and(tile < top_cols, row < top_rows), spots, n_top)
    view = add_top(spots, early, n_top)
    view = view.reshape(top_cols, 2 * top_rows, lanes)
    chips = n_col // 2
    my_chip, my_core = lax.axis_index("col") // 2, lax.axis_index("col") % 2
    top = jnp.zeros((chips,) + view.shape, jnp.float32)
    for step in range(chips):
        moved = view
        if step:
            hops = [(2 * i + k, 2 * ((i + step) % chips) + k) for i in range(chips) for k in range(2)]
            moved = lax.ppermute(view, "col", hops)
        origin = (my_chip + chips - step) % chips
        top = lax.dynamic_update_slice(top, moved[None], (origin, 0, 0, 0))
    top, first_pack = lax.optimization_barrier((top, first_pack))
    received0 = exchange(first_pack)
    top = lax.all_gather(top, "row").reshape(devices // 2, top_cols, 2 * top_rows, lanes)

    second_pack = pack_tiles(order, child_tiles, mask_columns, at + CHUNKS[0], CHUNKS[1])
    received0, second_pack = lax.optimization_barrier((received0, second_pack))
    received1 = exchange(second_pack)
    pieces = received0.reshape(devices, CHUNKS[0], 2, lanes)
    sums = add_pieces(targets, pieces, early, None, at, 16, BULK)
    top, sums = lax.optimization_barrier((top, sums))
    swap = [(i, i + 1 - 2 * (i % 2)) for i in range(n_col)]
    other_top = lax.ppermute(top, "col", swap)

    def near_corner(x):
        x = x.reshape(devices // 2, top_cols, n_col, col_blocks, 2, lanes)[:, :, :2, 0]
        return x.reshape(devices // 2, 1, 4 * top_cols, lanes)

    corner = jnp.where(
        my_core == jnp.arange(2).reshape(1, 2, 1, 1), near_corner(top), near_corner(other_top)
    )
    lower, inverse = factor_corner(corner.reshape(devices, 4 * top_cols, lanes), diagonal[:8])
    own_rows = lax.dynamic_slice(
        lower.reshape(top_cols, devices, top_cols * lanes),
        (0, me, 0),
        (top_cols, 1, top_cols * lanes),
    )
    own_rows = jnp.pad(own_rows.reshape(top_cols, top_cols * lanes), ((0, 8 - top_cols), (0, 0)))
    received1, inverse, own_rows = lax.optimization_barrier((received1, inverse, own_rows))
    pieces = received1.reshape(devices, CHUNKS[1], 2, lanes)
    sums = add_pieces(targets, pieces, None, sums, at + CHUNKS[0], 20, BULK)

    own = jnp.where(jnp.arange(lanes, dtype=jnp.int32)[None, :] == me, diagonal, 0.0)
    result = update_rows(
        my_core.reshape(1),
        sums.reshape(col_blocks, n_col, halves, 2 * row_tiles, lanes), top, other_top, inverse, own_rows, own
    )
    received = exchange(result.reshape(devices, -1, lanes))
    rows = place_rows(received)
    rows = rows.reshape(NF // n_row, halves, col_blocks, lanes).transpose(0, 2, 1, 3)
    return rows.reshape(NF // n_row, col_blocks, panel)


def solution(mesh):
    in_specs = (
        P(("row", "col"), None, None),
        P(("row", "col")),
        P(("row", "col"), None),
        P(("row", "col")),
        P(None, "col"),
    )
    out_specs = P("row", None, "col")
    return jax.shard_map(
        on_device, mesh=mesh, in_specs=in_specs, out_specs=out_specs, check_vma=False
    )
```

```python
import jax
import jax.numpy as jnp
from jax import lax
from jax.experimental import pallas as pl
from jax.experimental.pallas import tpu as pltpu
from jax.sharding import PartitionSpec as P

NF = 49152
EARLY = 8
GROUP = 8
CHUNKS = (64, 40)
BULK = 2**31
HIGHEST = lax.Precision.HIGHEST
VMEM_BYTES = 56 * 1024 * 1024


def pack_tiles(order, child_tiles, mask_columns, first, count, meta=None):
    tile_rows, tile_cols = child_tiles.shape[1:]
    stripes = tile_rows // 2
    base = first // GROUP
    extra = 0 if meta is None else meta.shape[0]
    width = 2 * GROUP + extra

    def body(order_ref, *refs):
        tiles, mask_ref = refs[:GROUP], refs[GROUP]
        out_ref, rows_ref = refs[-2], refs[-1]
        for i in range(GROUP):
            for s in range(2):
                rows = tiles[i][0, s * stripes : (s + 1) * stripes, :]
                column = mask_ref[0, s * stripes : (s + 1) * stripes, i : i + 1]
                rows_ref[pl.ds(2 * i + s, stripes, stride=2 * GROUP), :] = rows * column
        out_ref[:, : 2 * GROUP, :] = rows_ref[...].reshape(stripes, 2 * GROUP, tile_cols)
        if extra:
            meta_ref = refs[GROUP + 1]
            out_ref[:, 2 * GROUP :, :] = jnp.broadcast_to(
                meta_ref[...][None], (stripes, extra, tile_cols)
            )

    def tile_spec(i):
        return pl.BlockSpec(
            (1, tile_rows, tile_cols), lambda g, order_ref: (order_ref[first + g * GROUP + i], 0, 0)
        )

    in_specs = [tile_spec(i) for i in range(GROUP)]
    in_specs.append(pl.BlockSpec((1, tile_rows, GROUP), lambda g, order_ref: (base + g, 0, 0)))
    operands = [child_tiles] * GROUP + [mask_columns]
    if extra:
        in_specs.append(pl.BlockSpec((extra, tile_cols), lambda g, order_ref: (0, 0)))
        operands.append(meta)
    steps = count // GROUP
    return pl.pallas_call(
        body,
        grid_spec=pltpu.PrefetchScalarGridSpec(
            num_scalar_prefetch=1,
            grid=(steps,),
            in_specs=in_specs,
            out_specs=pl.BlockSpec((stripes, width, tile_cols), lambda g, order_ref: (0, g, 0)),
            scratch_shapes=[pltpu.VMEM((stripes * 2 * GROUP, tile_cols), jnp.float32)],
        ),
        out_shape=jax.ShapeDtypeStruct((stripes, steps * width, tile_cols), jnp.float32),
        compiler_params=pltpu.CompilerParams(vmem_limit_bytes=VMEM_BYTES),
        name="pack_tiles",
    )(order, *operands)


def add_pieces(targets, pieces, early, sums, first, window, weight):
    sources, count, two, lanes = pieces.shape
    n_sums = 6144
    per_step = 32
    fresh = sums is None

    def body(target_ref, pieces_ref, *refs):
        sums_ref = refs[-1]
        step = pl.program_id(0)

        @pl.when(step == 0)
        def _():
            sums_ref[...] = jnp.zeros_like(sums_ref) if fresh else refs[0][...]

        for n in range(per_step):
            source = step * per_step + n
            if fresh:
                for i in range(EARLY):
                    d = target_ref[source, i]
                    sums_ref[d] = sums_ref[d] + refs[0][n, i]
            for at in range(0, count, window):
                ds = [target_ref[source, first + at + i] for i in range(window)]
                news = [sums_ref[ds[i]] + pieces_ref[n, at + i] for i in range(window)]
                for i in range(window):
                    sums_ref[ds[i]] = news[i]

    def streamed(x):
        return pl.BlockSpec((per_step,) + x.shape[1:], lambda g, target_ref: (g, 0, 0, 0))

    whole = pl.BlockSpec(
        (n_sums, two, lanes), lambda g, target_ref: (0, 0, 0), pipeline_mode=pl.Buffered(1)
    )
    return pl.pallas_call(
        body,
        grid_spec=pltpu.PrefetchScalarGridSpec(
            num_scalar_prefetch=1,
            grid=(sources // per_step,),
            in_specs=[streamed(pieces), streamed(early) if fresh else whole],
            out_specs=whole,
        ),
        out_shape=jax.ShapeDtypeStruct((n_sums, two, lanes), jnp.float32),
        compiler_params=pltpu.CompilerParams(vmem_limit_bytes=VMEM_BYTES),
        cost_estimate=pl.CostEstimate(flops=weight, transcendentals=0, bytes_accessed=weight),
        name="add_pieces",
    )(targets, pieces, early if fresh else sums)


def add_top(spots, pieces, n_sums):
    sources, pitch, two, lanes = pieces.shape
    slots = spots.shape[1]

    def body(spot_ref, pieces_ref, out_ref, *parts):
        for part in parts:
            part[...] = jnp.zeros_like(part)

        def one(source, _):
            for i in range(slots):
                d = spot_ref[source, i]
                parts[i][d] = parts[i][d] + pieces_ref[source, i]
            return 0

        lax.fori_loop(0, sources, one, 0, unroll=4)
        total = parts[0][:n_sums]
        for part in parts[1:]:
            total = total + part[:n_sums]
        out_ref[...] = total

    return pl.pallas_call(
        body,
        grid_spec=pltpu.PrefetchScalarGridSpec(
            num_scalar_prefetch=1,
            grid=(1,),
            in_specs=[pl.BlockSpec(pieces.shape, lambda g, spot_ref: (0, 0, 0, 0))],
            out_specs=pl.BlockSpec((n_sums, two, lanes), lambda g, spot_ref: (0, 0, 0)),
            scratch_shapes=[pltpu.VMEM((n_sums + 8, two, lanes), jnp.float32)] * slots,
        ),
        out_shape=jax.ShapeDtypeStruct((n_sums, two, lanes), jnp.float32),
        compiler_params=pltpu.CompilerParams(vmem_limit_bytes=VMEM_BYTES),
        name="add_top",
    )(spots, pieces)


def factor_corner(corner, diagonal):
    size = corner.shape[2]
    n = 4

    def dot(a, b, transposed):
        dims = (((1,), (1 if transposed else 0,)), ((), ()))
        return lax.dot_general(a, b, dims, precision=HIGHEST, preferred_element_type=jnp.float32)

    def eliminate(block):
        groups = [block[8 * g : 8 * g + 8, :] for g in range(size // 8)]
        lane = lax.broadcasted_iota(jnp.int32, (8, size), 1)
        sub = lax.broadcasted_iota(jnp.int32, (8, size), 0)
        for p in range(size // 8):
            j0 = 8 * p
            rows = [jnp.broadcast_to(groups[p][r : r + 1, :], (8, size)) for r in range(8)]
            entry = [
                [
                    jnp.broadcast_to(rows[r][:, j0 + c : j0 + c + 1], (8, size)) if c >= r else None
                    for c in range(8)
                ]
                for r in range(8)
            ]
            ratio = [[None] * 8 for _ in range(8)]
            scaled = []
            done = groups[p]
            for r in range(8):
                row = jnp.where(jnp.logical_and(lane >= j0, lane < j0 + r), 0.0, rows[r])
                for q in range(r):
                    settled = jnp.logical_and(lane > j0 + q, lane < j0 + r)
                    row = row - ratio[r][q] * jnp.where(settled, 0.0, rows[q])
                done = jnp.where(sub == r, row, done)
                rows[r] = jnp.where(lane == j0 + r, 1.0, row)
                inverse = 1.0 / entry[r][r]
                settled = jnp.logical_and(lane > j0 + r, lane < j0 + 8)
                scaled.append(jnp.where(settled, 0.0, rows[r]) * inverse)
                for c in range(r + 1, 8):
                    ratio[c][r] = entry[r][c] * inverse
                for c in range(r + 1, 8):
                    for d in range(c, 8):
                        entry[c][d] = entry[c][d] - ratio[c][r] * entry[r][d]
            groups[p] = done
            inside = jnp.logical_and(lane >= j0, lane < j0 + 8)
            for g in range(p + 1, size // 8):
                columns = []
                result = jnp.where(inside, 0.0, groups[g])
                for c in range(8):
                    column = jnp.broadcast_to(groups[g][:, j0 + c : j0 + c + 1], (8, size))
                    for q in range(c):
                        column = column - ratio[c][q] * columns[q]
                    columns.append(column)
                    result = result - column * scaled[c]
                groups[g] = result
        return jnp.concatenate(groups, axis=0)

    def body(corner_ref, diag_ref, lower_ref, inverse_ref, flat_ref, a_ref, l_ref, i_ref):
        row = lax.broadcasted_iota(jnp.int32, (size, size), 0)
        col = lax.broadcasted_iota(jnp.int32, (size, size), 1)
        flat_ref[...] = corner_ref[...].reshape(size * 16, size)

        def raw(q, t):
            block = flat_ref[pl.ds(t * 4 + q, size, stride=16), :]
            if q == t:
                block = block + jnp.where(row == col, diag_ref[t : t + 1, :], 0.0)
            return block

        for q in range(n):
            for t in range(q + 1):
                block = raw(q, t)
                if q // 2 == t // 2:
                    block = 0.5 * (block + raw(t, q).T)
                a_ref[q * n + t] = block

        def step(k, _):
            done = eliminate(a_ref[k * n + k])
            pivots = jnp.sum(jnp.where(row == col, done, 0.0), axis=1, keepdims=True)
            root = jnp.sqrt(pivots)
            upper = jnp.where(col >= row, done, 0.0) / root
            inv = jnp.where(col < row, done, jnp.where(col == row, 1.0, 0.0)) / root
            l_ref[k * n + k] = upper.T
            i_ref[k * n + k] = inv
            for i in range(1, n):

                @pl.when(i > k)
                def _():
                    l_ref[i * n + k] = dot(a_ref[i * n + k], inv, True)

            for i in range(1, n):
                for j in range(1, i + 1):

                    @pl.when(j > k)
                    def _():
                        a_ref[i * n + j] = a_ref[i * n + j] - dot(
                            l_ref[i * n + k], l_ref[j * n + k], True
                        )

            return 0

        lax.fori_loop(0, n, step, 0)
        for i in range(n):
            for j in range(i):
                total = dot(l_ref[i * n + j], i_ref[j * n + j], False)
                for k in range(j + 1, i):
                    total = total + dot(l_ref[i * n + k], i_ref[k * n + j], False)
                i_ref[i * n + j] = -dot(i_ref[i * n + i], total, False)
        zero = jnp.zeros((size, size), jnp.float32)
        for i in range(n):
            for j in range(n):
                rows, cols = slice(i * size, (i + 1) * size), slice(j * size, (j + 1) * size)
                lower_ref[rows, cols] = l_ref[i * n + j] if j <= i else zero
                inverse_ref[rows, cols] = i_ref[i * n + j] if j <= i else zero

    shape = jax.ShapeDtypeStruct((n * size, n * size), jnp.float32)
    blocks = pltpu.VMEM((n * n, size, size), jnp.float32)
    return pl.pallas_call(
        body,
        out_shape=(shape, shape),
        scratch_shapes=[pltpu.VMEM((size * 16, size), jnp.float32), blocks, blocks, blocks],
        compiler_params=pltpu.CompilerParams(vmem_limit_bytes=VMEM_BYTES),
        name="factor_corner",
    )(corner, diagonal)


def update_rows(core, sums, top, other_top, inverse, own_rows, diagonal):
    blocks, n_col, halves, n_rows, lanes = sums.shape
    pairs, top_cols, _, _ = top.shape
    stripes = 2 * pairs
    near = top_cols * lanes
    n_row = stripes // n_col
    share = n_rows // 2 // n_row
    pair = 8 // (blocks * halves)

    def dot(a, b, transposed):
        dims = (((1,), (1 if transposed else 0,)), ((), ()))
        precision = HIGHEST if a.dtype == jnp.float32 else None
        return lax.dot_general(a, b, dims, precision=precision, preferred_element_type=jnp.float32)

    def body(
        core_ref,
        sums_ref,
        panel_in_ref,
        top_ref,
        other_ref,
        inverse_ref,
        own_ref,
        diag_ref,
        out_ref,
        panel_ref,
        high_ref,
        low_ref,
        flat_ref,
        result_ref,
        mixed_ref,
    ):
        g = pl.program_id(0)
        n_diag = diag_ref.shape[0]
        row = lax.broadcasted_iota(jnp.int32, (n_diag, lanes), 0)

        def with_diagonal(x, t):
            head = x[:n_diag] + jnp.where(row == t, diag_ref[...], 0.0)
            return jnp.concatenate([head, x[n_diag:]], axis=0)

        @pl.when(g == 0)
        def _():
            x = jnp.concatenate(
                [with_diagonal(panel_in_ref[0, t // 2, t % 2], t) for t in range(top_cols)], axis=1
            )
            panel = dot(x, inverse_ref[...], True)
            at = lax.broadcasted_iota(jnp.int32, (8, near), 0)
            head = jnp.where(at < 4, own_ref[...], panel[:8])
            panel = jnp.concatenate([head, panel[8:]], axis=0)
            panel_ref[...] = panel
            factor = dot(panel, inverse_ref[...], False)
            high_ref[...] = factor.astype(jnp.bfloat16)
            low_ref[...] = (factor - high_ref[...].astype(jnp.float32)).astype(jnp.bfloat16)

        mine, theirs = top_ref[...], other_ref[...]
        first = core_ref[0] == 0
        both = [jnp.where(first, mine, theirs), jnp.where(first, theirs, mine)]
        both = [x.reshape(pairs, 1, top_cols * 8, lanes) for x in both]
        flat_ref[...] = jnp.concatenate(both, axis=1).reshape(stripes * top_cols * 8, lanes)
        for i in range(pair):
            c = g * pair + i
            for cb in range(blocks):
                weights = jnp.concatenate(
                    [
                        jnp.concatenate(
                            [
                                flat_ref[
                                    pl.ds(
                                        k * 8 + (i * blocks + cb) * halves + h,
                                        stripes,
                                        stride=top_cols * 8,
                                    ),
                                    :,
                                ]
                                for k in range(top_cols)
                            ],
                            axis=1,
                        )
                        for h in range(halves)
                    ],
                    axis=0,
                )
                high = weights.astype(jnp.bfloat16)
                low = (weights - high.astype(jnp.float32)).astype(jnp.bfloat16)
                product = dot(low_ref[...], high, True) + dot(high_ref[...], low, True)
                product = product + dot(high_ref[...], high, True)
                for h in range(halves):
                    t = (cb * n_col + c) * halves + h
                    result = with_diagonal(sums_ref[cb, i, h], t)
                    result = result - product[:, h * lanes : (h + 1) * lanes]
                    if cb == 0:
                        at = (i * halves + h) * lanes
                        result = jnp.where(g == 0, panel_ref[:, at : at + lanes], result)
                    result_ref[...] = result
                    for s in range(2):
                        mixed_ref[pl.ds(s * 4 + h * 2 + cb, n_rows // 2, stride=8), :] = result_ref[
                            pl.ds(s, n_rows // 2, stride=2), :
                        ]
            out_ref[:, i] = mixed_ref[...].reshape(n_row, share * 8, lanes)

    def fixed(*shape):
        return pl.BlockSpec(shape, lambda g, core_ref: (0,) * len(shape))

    top_spec = pl.BlockSpec((pairs, top_cols, 8, lanes), lambda g, core_ref: (0, 0, g, 0))
    return pl.pallas_call(
        body,
        grid_spec=pltpu.PrefetchScalarGridSpec(
            num_scalar_prefetch=1,
            grid=(n_col // pair,),
            in_specs=[
                pl.BlockSpec(
                    (blocks, pair, halves, n_rows, lanes), lambda g, core_ref: (0, g, 0, 0, 0)
                ),
                pl.BlockSpec((1, 2, halves, n_rows, lanes), lambda g, core_ref: (0, 0, 0, 0, 0)),
                top_spec,
                top_spec,
                fixed(near, near),
                fixed(8, near),
                fixed(*diagonal.shape),
            ],
            out_specs=pl.BlockSpec(
                (n_row, pair, share * 8, lanes), lambda g, core_ref: (0, g, 0, 0)
            ),
            scratch_shapes=[
                pltpu.VMEM((n_rows, near), jnp.float32),
                pltpu.VMEM((n_rows, near), jnp.bfloat16),
                pltpu.VMEM((n_rows, near), jnp.bfloat16),
                pltpu.VMEM((stripes * top_cols * 8, lanes), jnp.float32),
                pltpu.VMEM((n_rows, lanes), jnp.float32),
                pltpu.VMEM((n_rows * 4, lanes), jnp.float32),
            ],
        ),
        out_shape=jax.ShapeDtypeStruct((n_row, n_col, share * 8, lanes), jnp.float32),
        compiler_params=pltpu.CompilerParams(vmem_limit_bytes=VMEM_BYTES),
        name="update_rows",
    )(core, sums, sums, top, other_top, inverse, own_rows, diagonal)


def place_rows(received):
    stripes, width, lanes = received.shape
    units = width // 4
    share = units // 2

    def body(in_ref, out_ref):
        for s in range(share):
            out_ref[s] = in_ref[:, s]

    return pl.pallas_call(
        body,
        grid=(units // share,),
        in_specs=[pl.BlockSpec((stripes, share, 4, lanes), lambda g: (0, g, 0, 0))],
        out_specs=pl.BlockSpec((share, stripes, 4, lanes), lambda g: (g, 0, 0, 0)),
        out_shape=jax.ShapeDtypeStruct((units, stripes, 4, lanes), jnp.float32),
        compiler_params=pltpu.CompilerParams(vmem_limit_bytes=VMEM_BYTES),
        name="place_rows",
    )(received.reshape(stripes, units, 4, lanes))


def tile_order(tile_dest, col_tiles, top_rows, top_cols):
    total = tile_dest.shape[0]
    ids = jnp.arange(total, dtype=jnp.int32)
    same = tile_dest[:, None] == tile_dest[None, :]
    first_of = jnp.min(jnp.where(same, ids[None, :], total), axis=1)
    later = jnp.any(jnp.logical_and(same, ids[None, :] > ids[:, None]), axis=1)
    top = jnp.logical_and(tile_dest // col_tiles < top_rows, tile_dest % col_tiles < top_cols)
    rest = jnp.where(
        first_of < ids, 3 * total + first_of, jnp.where(later, total + ids, 2 * total + ids)
    )
    key = jnp.where(top, ids, rest)
    position = jnp.sum((key[None, :] < key[:, None]).astype(jnp.int32), axis=1)
    return (position[:, None] == ids[None, :]).astype(jnp.int32)


def on_device(child_tiles, tile_dest, tile_mask, tile_count, front_diagonal):
    axes = ("row", "col")
    n_row = lax.axis_size("row")
    n_col = lax.axis_size("col")
    devices = n_row * n_col
    me = lax.axis_index("row") * n_col + lax.axis_index("col")
    tile_total, tile_rows, lanes = child_tiles.shape
    col_blocks, panel = front_diagonal.shape
    halves = panel // lanes
    row_tiles = NF // tile_rows
    col_tiles = col_blocks * n_col * halves
    width = col_tiles * lanes
    top_rows = width // tile_rows
    top_cols = 2 * halves

    placed = tile_order(tile_dest, col_tiles, top_rows, top_cols)
    ids = jnp.arange(tile_total, dtype=jnp.int32)
    target = (tile_dest % col_tiles) * row_tiles + tile_dest // col_tiles
    order = jnp.sum(placed * ids[:, None], axis=0)
    target_sent = jnp.sum(placed * target[:, None], axis=0)
    live = (ids < tile_count[0]).astype(jnp.float32)
    mask_columns = lax.dot_general(
        tile_mask.astype(jnp.float32),
        placed.astype(jnp.float32) * live[:, None],
        (((0,), (0,)), ((), ())),
    )
    mask_columns = mask_columns.reshape(tile_rows, tile_total // GROUP, GROUP).transpose(1, 0, 2)
    meta = jnp.concatenate(
        [
            jnp.pad(target_sent.astype(jnp.float32), (0, lanes - tile_total))[None],
            front_diagonal.reshape(col_blocks * halves, lanes),
            jnp.zeros((8 - 1 - col_blocks * halves, lanes), jnp.float32),
        ],
        axis=0,
    )

    def exchange(x):
        return lax.all_to_all(x, axes, split_axis=0, concat_axis=0, tiled=True)

    early = exchange(pack_tiles(order, child_tiles, mask_columns, 0, EARLY, meta))
    at = EARLY
    first_pack = pack_tiles(order, child_tiles, mask_columns, at, CHUNKS[0])
    early, first_pack = lax.optimization_barrier((early, first_pack))

    targets = early[:, 2 * EARLY, :].astype(jnp.int32)
    diagonal = early[:n_col, 2 * EARLY + 1 : 2 * EARLY + 1 + col_blocks * halves, :]
    diagonal = diagonal.reshape(n_col, col_blocks, panel).transpose(1, 0, 2)
    diagonal = diagonal.reshape(col_tiles, lanes)
    early = early.reshape(devices, EARLY + 4, 2, lanes)
    n_top = top_cols * top_rows
    tile, row = targets[:, :EARLY] // row_tiles, targets[:, :EARLY] % row_tiles
    spots = tile * top_rows + row % n_col * col_blocks + row // n_col
    spots = jnp.where(jnp.logical_and(tile < top_cols, row < top_rows), spots, n_top)
    view = add_top(spots, early, n_top)
    view = view.reshape(top_cols, 2 * top_rows, lanes)
    chips = n_col // 2
    my_chip, my_core = lax.axis_index("col") // 2, lax.axis_index("col") % 2
    top = jnp.zeros((chips,) + view.shape, jnp.float32)
    for step in range(chips):
        moved = view
        if step:
            hops = [(2 * i + k, 2 * ((i + step) % chips) + k) for i in range(chips) for k in range(2)]
            moved = lax.ppermute(view, "col", hops)
        origin = (my_chip + chips - step) % chips
        top = lax.dynamic_update_slice(top, moved[None], (origin, 0, 0, 0))
    top, first_pack = lax.optimization_barrier((top, first_pack))
    received0 = exchange(first_pack)
    top = lax.all_gather(top, "row").reshape(devices // 2, top_cols, 2 * top_rows, lanes)

    second_pack = pack_tiles(order, child_tiles, mask_columns, at + CHUNKS[0], CHUNKS[1])
    received0, second_pack = lax.optimization_barrier((received0, second_pack))
    received1 = exchange(second_pack)
    pieces = received0.reshape(devices, CHUNKS[0], 2, lanes)
    sums = add_pieces(targets, pieces, early, None, at, 16, BULK)
    top, sums = lax.optimization_barrier((top, sums))
    swap = [(i, i + 1 - 2 * (i % 2)) for i in range(n_col)]
    other_top = lax.ppermute(top, "col", swap)

    def near_corner(x):
        x = x.reshape(devices // 2, top_cols, n_col, col_blocks, 2, lanes)[:, :, :2, 0]
        return x.reshape(devices // 2, 1, 4 * top_cols, lanes)

    corner = jnp.where(
        my_core == jnp.arange(2).reshape(1, 2, 1, 1), near_corner(top), near_corner(other_top)
    )
    lower, inverse = factor_corner(corner.reshape(devices, 4 * top_cols, lanes), diagonal[:8])
    own_rows = lax.dynamic_slice(
        lower.reshape(top_cols, devices, top_cols * lanes),
        (0, me, 0),
        (top_cols, 1, top_cols * lanes),
    )
    own_rows = jnp.pad(own_rows.reshape(top_cols, top_cols * lanes), ((0, 8 - top_cols), (0, 0)))
    received1, inverse, own_rows = lax.optimization_barrier((received1, inverse, own_rows))
    pieces = received1.reshape(devices, CHUNKS[1], 2, lanes)
    sums = add_pieces(targets, pieces, None, sums, at + CHUNKS[0], 20, BULK)

    own = jnp.where(jnp.arange(lanes, dtype=jnp.int32)[None, :] == me, diagonal, 0.0)
    result = update_rows(
        my_core.reshape(1),
        sums.reshape(col_blocks, n_col, halves, 2 * row_tiles, lanes), top, other_top, inverse, own_rows, own
    )
    received = exchange(result.reshape(devices, -1, lanes))
    rows = place_rows(received)
    rows = rows.reshape(NF // n_row, halves, col_blocks, lanes).transpose(0, 2, 1, 3)
    return rows.reshape(NF // n_row, col_blocks, panel)


def solution(mesh):
    in_specs = (
        P(("row", "col"), None, None),
        P(("row", "col")),
        P(("row", "col"), None),
        P(("row", "col")),
        P(None, "col"),
    )
    out_specs = P("row", None, "col")
    return jax.shard_map(
        on_device, mesh=mesh, in_specs=in_specs, out_specs=out_specs, check_vma=False
    )
```
